256 devices in a mesh: tile: 64 (over z, y_lo, x), mode: 4 (over y_hi, core).
Axes of the slice: x: 4, y: 4 (y_hi: 2, y_lo: 2; y = y_hi * 2 + y_lo), z: 8, core: 2. Of those that a mesh axis runs over, the one named last changes fastest.
Arguments:
- object_tiles: float32 [64, 2, 2, 256, 256], P('tile'), may hold values from -6 to 6
- object_previous: float32 [64, 2, 2, 256, 256], P('tile'), may hold values from -6 to 6
- probe: float32 [4, 8, 2, 256, 256], P(None, 'mode', None, 'tile'), may hold values from -2 to 2
- probe_previous: float32 [4, 8, 2, 256, 256], P(None, 'mode', None, 'tile'), may hold values from -6 to 6
- patterns: float32 [128, 256, 256], P('tile'), may hold values from 0 to 2
- offsets: int32 [2, 128], P(None, 'tile'), may hold values from 0 to 255
- scan_of_slot: int32 [128], P('tile'), may hold values from 0 to 3
- tile_load: int32 [64], P('tile'), may hold values from 1 to 2, as said below
- step_sizes: int32 [2], replicated, may hold values from 128 to 511
- object_norm_before: float32 [1], replicated, may hold values from 0.1 to 0.4
- probe_norm_before: float32 [1], replicated, may hold values from 12 to 64
Outputs:
- new_object: float32 [64, 2, 2, 256, 256], P('tile')
- object_direction: float32 [64, 2, 2, 256, 256], P('tile')
- new_probe: float32 [4, 8, 2, 256, 256], P(None, 'mode', None, 'tile')
- probe_direction: float32 [4, 8, 2, 256, 256], P(None, 'mode', None, 'tile')
The draws below stay inside these ranges and needn't reach their ends.
Inputs may be any that keep to these rules, and one draw needn't show every extreme that they name: `tile_load`: every tile holds 1 to 2 used slots, and some tile holds exactly 2.
All inputs are finite; a program needn't handle non-finite values.
Results may differ from the reference program's by a relative error of at most 0.024.
Values may be sent and summed in bfloat16 or wider, within the bound.
No kernel may reach another device: no remote copies, remote signals or barrier semaphores. Data moves between devices by JAX's collectives and lax.ppermute only.
A program may use at most 64 MiB of HBM per device.

```python
import math
import jax
import jax.numpy as jnp
from jax import lax

PATTERN_SIDE = 256
TILE_WIDTH = 256
TGX = 8
LAYERS = 2
MODES = 8
SCAN_COUNT = 4
CAP = 2
TILES = 64
SLOT_COUNT = 128
N_TILE = 64


def draw_tile_load(key, part):
    first_key, second_key = jax.random.split(jax.random.fold_in(key, 7))
    level = jax.random.randint(first_key, (TILES,), 0, 16)
    loads = jnp.where(level == 0, CAP, jnp.where(level == 1, 2, 1))
    chosen = jax.random.randint(second_key, (), 0, TILES)
    return jnp.where(jnp.arange(TILES) == chosen, CAP, loads).astype(jnp.int32)


def place_ends(entries, key, low, top_value):
    index_at = [jax.random.randint(jax.random.fold_in(key, axis), (), 0, length) for axis, length in enumerate(entries.shape)]
    longest = entries.shape.index(max(entries.shape))
    next_to = index_at[:longest] + [(index_at[longest] + 1) % entries.shape[longest]] + index_at[longest + 1:]
    return entries.at[tuple(index_at)].set(low).at[tuple(next_to)].set(top_value)


def steps_of(own_key, dims, cuts, smallest, top_value):
    factor_of, own = 1.0, jax.random.fold_in(own_key, 6)
    for position, shards_of in cuts:
        heights = jnp.exp(jax.random.uniform(jax.random.fold_in(own, position), (shards_of,), jnp.float32, smallest / len(cuts), top_value / len(cuts)))
        factor_of = factor_of * jnp.repeat(heights, dims[position] // shards_of).reshape([-1 if axis == position else 1 for axis in range(len(dims))])
    return factor_of


def normal_values(key, extent, width, bound, shards=(), kind=jnp.bfloat16):
    factor_of = steps_of(key, extent, shards, -0.22, 0.18) if shards else 1.0
    values = jax.random.normal(key, extent, jnp.float32) * width * factor_of
    return jnp.minimum(jnp.maximum(values, -bound), bound).astype(kind)


def setup_inputs(seed: int = 0) -> dict:
    key_list = jax.random.split(jax.random.key(seed), 12)
    return {
        "object_tiles": normal_values(key_list[0], (TILES, LAYERS, 2, TILE_WIDTH, TILE_WIDTH), 1.0, 6.0, ((0, 64),), jnp.float32),
        "object_previous": normal_values(key_list[1], (TILES, LAYERS, 2, TILE_WIDTH, TILE_WIDTH), 0.5, 6.0, ((0, 64),), jnp.float32),
        "probe": normal_values(key_list[2], (SCAN_COUNT, MODES, 2, PATTERN_SIDE, PATTERN_SIDE), 0.125, 2.0, ((1, 4), (3, 64)), jnp.float32),
        "probe_previous": normal_values(key_list[3], (SCAN_COUNT, MODES, 2, PATTERN_SIDE, PATTERN_SIDE), 1.0, 6.0, ((1, 4), (3, 64)), jnp.float32),
        "patterns": jnp.clip(2.0 * jax.random.uniform(key_list[4], (SLOT_COUNT, PATTERN_SIDE, PATTERN_SIDE), jnp.float32) ** steps_of(key_list[4], (SLOT_COUNT, PATTERN_SIDE, PATTERN_SIDE), ((0, 64),), -0.2, 0.2), 0.0, 2.0),
        "offsets": place_ends(jax.random.randint(key_list[5], (2, SLOT_COUNT), 0, TILE_WIDTH), jax.random.fold_in(key_list[5], 1), 0, TILE_WIDTH - 1).astype(jnp.int32),
        "scan_of_slot": place_ends(jax.random.randint(key_list[6], (SLOT_COUNT,), 0, SCAN_COUNT), jax.random.fold_in(key_list[6], 1), 0, SCAN_COUNT - 1).astype(jnp.int32),
        "tile_load": draw_tile_load(jax.random.fold_in(key_list[11], 71), 0),
        "step_sizes": jax.random.randint(key_list[8], (2,), 128, 512).astype(jnp.int32),
        "object_norm_before": jnp.clip(jnp.exp(jax.random.uniform(key_list[9], (1,), jnp.float32, math.log(0.1), math.log(0.4))), 0.1, 0.4),
        "probe_norm_before": jnp.clip(jnp.exp(jax.random.uniform(key_list[10], (1,), jnp.float32, math.log(12.0), math.log(64.0))), 12.0, 64.0),
    }


residual_weight = 2.0

def table_pair():
    index_row = jnp.arange(PATTERN_SIDE, dtype=jnp.int32)
    product = index_row[:, None] * index_row[None, :] % PATTERN_SIDE
    angle = product.astype(jnp.float32) * (2.0 * math.pi / PATTERN_SIDE)
    factor = 1.0 / math.sqrt(PATTERN_SIDE)
    cosine = (jnp.cos(angle) * factor).astype(jnp.bfloat16)
    sine = (-jnp.sin(angle) * factor).astype(jnp.bfloat16)
    index_free = jnp.where(index_row < PATTERN_SIDE // 2, index_row, index_row - PATTERN_SIDE).astype(jnp.float32)
    phase = (index_free[:, None] * index_free[:, None] + index_free[None, :] * index_free[None, :]) * (math.pi / (4.0 * PATTERN_SIDE))
    return (cosine, sine, jnp.cos(phase), jnp.sin(phase))

def right_product(left_data, table):
    return jnp.einsum('...jk,kl->...jl', left_data.astype(jnp.float32), table.astype(jnp.float32), precision=lax.Precision.HIGHEST)

def left_product(table, right_data):
    return jnp.einsum('ij,...jl->...il', table.astype(jnp.float32), right_data.astype(jnp.float32), precision=lax.Precision.HIGHEST)

def transform(wave_re, wave_im, tables, inverse):
    cosine = tables[0]
    sine = -tables[1] if inverse else tables[1]
    first_re = (right_product(wave_re, cosine) - right_product(wave_im, sine)).astype(jnp.bfloat16)
    first_im = (right_product(wave_re, sine) + right_product(wave_im, cosine)).astype(jnp.bfloat16)
    out_re = (left_product(cosine, first_re) - left_product(sine, first_im)).astype(jnp.bfloat16)
    out_im = (left_product(sine, first_re) + left_product(cosine, first_im)).astype(jnp.bfloat16)
    return (out_re, out_im)

def complex_times(first_re, first_im, second_re, second_im):
    first_portion = first_re.astype(jnp.float32)
    b_part = first_im.astype(jnp.float32)
    c_part = second_re.astype(jnp.float32)
    d_part = second_im.astype(jnp.float32)
    return (first_portion * c_part - b_part * d_part, first_portion * d_part + b_part * c_part)

def conj_times(first_re, first_im, second_re, second_im):
    first_portion = first_re.astype(jnp.float32)
    b_part = first_im.astype(jnp.float32)
    c_part = second_re.astype(jnp.float32)
    d_part = second_im.astype(jnp.float32)
    return (first_portion * c_part + b_part * d_part, first_portion * d_part - b_part * c_part)

def propagate(wave_re, wave_im, tables, adjoint):
    spec_re, spec_im = transform(wave_re, wave_im, tables, False)
    kernel_im = -tables[3] if adjoint else tables[3]
    moved_re, moved_im = complex_times(spec_re, spec_im, tables[2], kernel_im)
    return transform(moved_re.astype(jnp.bfloat16), moved_im.astype(jnp.bfloat16), tables, True)

def one_slot(patch_data, probe_modes, measured, valid_mask, tables):
    wave_re = probe_modes[:, 0]
    wave_im = probe_modes[:, 1]
    incident = []
    for layer_index in range(LAYERS):
        incident.append((wave_re, wave_im))
        next_re, next_im = complex_times(wave_re, wave_im, patch_data[layer_index, 0], patch_data[layer_index, 1])
        wave_re = next_re.astype(jnp.bfloat16)
        wave_im = next_im.astype(jnp.bfloat16)
        if layer_index + 1 < LAYERS:
            wave_re, wave_im = propagate(wave_re, wave_im, tables, False)
    far_re, far_im = transform(wave_re, wave_im, tables, False)
    far_re32 = far_re.astype(jnp.float32)
    far_im32 = far_im.astype(jnp.float32)
    power = lax.optimization_barrier(jnp.sum(far_re32 * far_re32 + far_im32 * far_im32, axis=0))
    misfit = (power - measured) * valid_mask
    back_re = (residual_weight * misfit[None] * far_re32).astype(jnp.bfloat16)
    back_im = (residual_weight * misfit[None] * far_im32).astype(jnp.bfloat16)
    back_re, back_im = transform(back_re, back_im, tables, True)
    slice_terms = [None] * LAYERS
    probe_terms = None
    for layer_index in reversed(range(LAYERS)):
        inc_re, inc_im = incident[layer_index]
        grad_re, grad_im = conj_times(inc_re, inc_im, back_re, back_im)
        slice_terms[layer_index] = jnp.stack([lax.optimization_barrier(jnp.sum(grad_re, axis=0)), lax.optimization_barrier(jnp.sum(grad_im, axis=0))], axis=0)
        carry_re, carry_im = conj_times(patch_data[layer_index, 0], patch_data[layer_index, 1], back_re, back_im)
        if layer_index > 0:
            back_re, back_im = propagate(carry_re.astype(jnp.bfloat16), carry_im.astype(jnp.bfloat16), tables, True)
        else:
            probe_terms = jnp.stack([carry_re, carry_im], axis=1)
    return (jnp.stack(slice_terms, axis=0), probe_terms)

def reference(object_tiles, object_previous, probe, probe_previous, patterns, offsets, scan_of_slot, tile_load, step_sizes, object_norm_before, probe_norm_before):
    extra = TGX + 1
    padded_tiles = jnp.concatenate([object_tiles.astype(jnp.bfloat16), jnp.zeros((extra, LAYERS, 2, TILE_WIDTH, TILE_WIDTH), jnp.bfloat16)], axis=0)
    probe_bf16 = probe.astype(jnp.bfloat16)
    tables = table_pair()
    anchor = jnp.zeros((), jnp.int32)

    def fetch(index):
        return lax.dynamic_index_in_dim(padded_tiles, index, 0, keepdims=False)

    def step(carry, slot_index):
        object_grad, probe_grad = carry
        tile_index = (slot_index // CAP).astype(jnp.int32)
        valid_mask = (slot_index % CAP < tile_load[tile_index]).astype(jnp.float32)
        upper = jnp.concatenate([fetch(tile_index), fetch(tile_index + 1)], axis=3)
        lower = jnp.concatenate([fetch(tile_index + TGX), fetch(tile_index + TGX + 1)], axis=3)
        region = jnp.concatenate([upper, lower], axis=2)
        starts = (anchor, anchor, offsets[0, slot_index].astype(jnp.int32), offsets[1, slot_index].astype(jnp.int32))
        patch_data = lax.dynamic_slice(region, starts, (LAYERS, 2, PATTERN_SIDE, PATTERN_SIDE))
        scan_index = scan_of_slot[slot_index]
        probe_modes = lax.dynamic_index_in_dim(probe_bf16, scan_index, 0, keepdims=False)
        measured = lax.dynamic_index_in_dim(patterns, slot_index, 0, keepdims=False)
        slice_terms, probe_terms = one_slot(patch_data, probe_modes, measured, valid_mask, tables)
        region_grad = jnp.zeros((LAYERS, 2, 2 * TILE_WIDTH, 2 * TILE_WIDTH), jnp.float32)
        region_grad = lax.dynamic_update_slice(region_grad, slice_terms, starts)
        quarters = ((tile_index, region_grad[:, :, :TILE_WIDTH, :TILE_WIDTH]), (tile_index + 1, region_grad[:, :, :TILE_WIDTH, TILE_WIDTH:]), (tile_index + TGX, region_grad[:, :, TILE_WIDTH:, :TILE_WIDTH]), (tile_index + TGX + 1, region_grad[:, :, TILE_WIDTH:, TILE_WIDTH:]))
        for target, piece in quarters:
            current = lax.dynamic_index_in_dim(object_grad, target, 0, keepdims=True)
            object_grad = lax.dynamic_update_slice_in_dim(object_grad, current + piece[None], target, 0)
        probe_grad = probe_grad.at[scan_index].add(probe_terms)
        return ((object_grad, probe_grad), None)
    object_init = jnp.zeros((N_TILE + extra, LAYERS, 2, TILE_WIDTH, TILE_WIDTH), jnp.float32)
    probe_init = jnp.zeros((SCAN_COUNT, MODES, 2, PATTERN_SIDE, PATTERN_SIDE), jnp.float32)
    (object_grad, probe_grad), _ = lax.scan(step, (object_init, probe_init), jnp.arange(N_TILE * CAP, dtype=jnp.int32))
    object_gradient = object_grad[:N_TILE]
    object_square = jnp.sum(object_gradient * object_gradient) / float(N_TILE * LAYERS * 2 * TILE_WIDTH * TILE_WIDTH)
    probe_square = jnp.sum(probe_grad * probe_grad) / float(SCAN_COUNT * MODES * 2 * PATTERN_SIDE * PATTERN_SIDE)
    object_direction = -object_gradient + object_square / object_norm_before[0] * object_previous
    new_object = object_tiles + step_sizes[0].astype(jnp.float32) / 1024.0 * object_direction
    probe_direction = -probe_grad + probe_square / probe_norm_before[0] * probe_previous
    new_probe = probe + step_sizes[1].astype(jnp.float32) / 16384.0 * probe_direction
    return (new_object, object_direction, new_probe, probe_direction)
```

```python
import functools
import math

import jax
import jax.numpy as jnp
import numpy as np
from jax import lax
from jax.experimental import pallas as pl
from jax.experimental.pallas import tpu as pltpu
from jax.sharding import Mesh, PartitionSpec as P

TGX = 8
LAYERS = 2
MODES = 8
SCANS = 4
W = 256
NZ, NYL, NX, NYH, NC = 8, 2, 4, 2, 2
NYLX = NYL * NX
TILES = NZ * NYLX
ROWS = W // TILES
BAND = NYLX * ROWS
TILE_AXES = ("z", "yl", "x")
PLANE = ("yl", "x", "yh")
VMEM = pltpu.VMEM
F32 = jnp.float32
BF16 = jnp.bfloat16


def tables():
    index = np.arange(W, dtype=np.int64)
    angle = ((index[:, None] * index[None, :]) % W).astype(np.float32) * np.float32(2.0 * math.pi / W)
    factor = np.float32(1.0 / math.sqrt(W))
    cosine = np.cos(angle, dtype=np.float32) * factor
    sine = -np.sin(angle, dtype=np.float32) * factor
    plus = np.block([[cosine, sine], [-sine, cosine]])
    minus = np.block([[cosine, -sine], [sine, cosine]])
    free = np.where(index < W // 2, index, index - W).astype(np.float32)
    phase = (free[:, None] * free[:, None] + free[None, :] * free[None, :]) * np.float32(math.pi / (4.0 * W))
    kernel = np.stack([np.cos(phase, dtype=np.float32), np.sin(phase, dtype=np.float32)])
    rows = np.arange(128)
    band, i, ri, r = rows // 16, rows // 8 % 2, rows // 4 % 2, rows % 4
    natural = i * 64 + ri * 32 + band * 4 + r
    order = np.zeros((128, 128), np.float32)
    order[natural, rows] = 1.0
    return plus, minus, kernel, order


def mm(a, b):
    return jnp.dot(a, b, preferred_element_type=F32)


def transform(wave_re, wave_im, right, left):
    across = jnp.concatenate([wave_re, wave_im], axis=1)
    first = mm(across, right).astype(BF16)
    down = jnp.concatenate([first[:, :W], first[:, W:]], axis=0)
    out = mm(left, down).astype(BF16)
    return out[:W], out[W:]


def times(a_re, a_im, b_re, b_im):
    a_re, a_im, b_re, b_im = (v.astype(F32) for v in (a_re, a_im, b_re, b_im))
    return a_re * b_re - a_im * b_im, a_re * b_im + a_im * b_re


def conj_times(a_re, a_im, b_re, b_im):
    a_re, a_im, b_re, b_im = (v.astype(F32) for v in (a_re, a_im, b_re, b_im))
    return a_re * b_re + a_im * b_im, a_re * b_im - a_im * b_re


def window_masks(row, col):
    rows = lax.broadcasted_iota(jnp.int32, (W, W), 0)
    cols = lax.broadcasted_iota(jnp.int32, (W, W), 1)
    return rows >= row, cols >= col


def patch_kernel(info, own, east, south, corner, out):
    row, col = info[0], info[1]
    upper, left = window_masks(row, col)
    for ri in range(2):
        top = jnp.where(left, own[ri].astype(F32), east[ri].astype(F32))
        low = jnp.where(left, south[ri].astype(F32), corner[ri].astype(F32))
        value = jnp.where(upper, top, low)
        value = pltpu.roll(value, (W - row) % W, 0)
        value = pltpu.roll(value, (W - col) % W, 1)
        out[ri] = value.astype(BF16)


def pick_kernel(ids, src, out):
    for d in range(NYLX * NYH):
        out[d] = src[:, ids[d]]


def forward_kernel(info, blocks, mine, other, plus, minus, kern, order, psi, inc, far, power):
    step = pl.program_id(0)
    first = info[2] == 0
    for z in range(NZ):
        piece = blocks[:, 0, z].reshape(128, W)
        placed = mm(order[...], piece).astype(BF16)
        for i in range(2):
            for ri in range(2):
                at = i * 64 + ri * 32
                psi[i, ri, z * BAND : (z + 1) * BAND] = placed[at : at + BAND]
    fwd, inv = plus[...], minus[...]
    p0 = [jnp.where(first, mine[ri], other[ri]) for ri in range(2)]
    p1 = [jnp.where(first, other[ri], mine[ri]) for ri in range(2)]
    total = None
    for i in range(2):
        e_re, e_im = times(psi[i, 0], psi[i, 1], p0[0], p0[1])
        s_re, s_im = transform(e_re.astype(BF16), e_im.astype(BF16), fwd, inv)
        m_re, m_im = times(s_re, s_im, kern[0], kern[1])
        w_re, w_im = transform(m_re.astype(BF16), m_im.astype(BF16), inv, fwd)
        inc[i, 0] = w_re
        inc[i, 1] = w_im
        e_re, e_im = times(w_re, w_im, p1[0], p1[1])
        f_re, f_im = transform(e_re.astype(BF16), e_im.astype(BF16), fwd, inv)
        far[i, 0] = f_re
        far[i, 1] = f_im
        f_re, f_im = f_re.astype(F32), f_im.astype(F32)
        part = f_re * f_re + f_im * f_im
        total = part if total is None else total + part

    @pl.when(step == 0)
    def _():
        power[...] = total

    @pl.when(step != 0)
    def _():
        power[...] += total


def backward_kernel(
    info, psi, inc, far, power_a, power_b, pattern, mine, other, plus, minus, kern, order, terms, out, scratch
):
    step = pl.program_id(0)
    core = info[2]
    first = core == 0
    used = info[4].astype(F32)
    fwd, inv = plus[...], minus[...]
    p0 = [jnp.where(first, mine[ri], other[ri]) for ri in range(2)]
    p1 = [jnp.where(first, other[ri], mine[ri]) for ri in range(2)]
    double = 2.0 * ((power_a[...] + power_b[...] - pattern[0]) * used)
    sums = [None] * 4
    for i in range(2):
        b_re = (double * far[i, 0].astype(F32)).astype(BF16)
        b_im = (double * far[i, 1].astype(F32)).astype(BF16)
        b_re, b_im = transform(b_re, b_im, inv, fwd)
        t1 = conj_times(inc[i, 0], inc[i, 1], b_re, b_im)
        c_re, c_im = conj_times(p1[0], p1[1], b_re, b_im)
        s_re, s_im = transform(c_re.astype(BF16), c_im.astype(BF16), fwd, inv)
        m_re, m_im = times(s_re, s_im, kern[0], -kern[1])
        b_re, b_im = transform(m_re.astype(BF16), m_im.astype(BF16), inv, fwd)
        t0 = conj_times(psi[i, 0], psi[i, 1], b_re, b_im)
        c_re, c_im = conj_times(p0[0], p0[1], b_re, b_im)
        scratch[i, 0] = c_re.astype(BF16)
        scratch[i, 1] = c_im.astype(BF16)
        new = [t0[0], t0[1], t1[0], t1[1]]
        sums = [n if s is None else s + n for s, n in zip(sums, new)]
    back = order[...].T
    for z in range(NZ):
        pieces = [
            scratch[i, ri, z * BAND : (z + 1) * BAND] for i in range(2) for ri in range(2)
        ]
        piece = mm(back, jnp.concatenate(pieces, axis=0)).astype(BF16)
        out[:, 0, z] = piece.reshape(NYLX, 16, W)
    for layer in range(LAYERS):
        slot = core if layer == 0 else 1 - core

        @pl.when(step == 0)
        def _():
            terms[slot, 0] = sums[2 * layer]
            terms[slot, 1] = sums[2 * layer + 1]

        @pl.when(step != 0)
        def _():
            terms[slot, 0] += sums[2 * layer]
            terms[slot, 1] += sums[2 * layer + 1]


def place_kernel(info, mine, theirs, own, right, below, corner):
    row, col = info[0], info[1]
    upper, left = window_masks(row, col)
    zero = jnp.zeros((W, W), F32)
    for ri in range(2):
        value = mine[ri] + theirs[ri].astype(F32)
        value = pltpu.roll(value, row, 0)
        value = pltpu.roll(value, col, 1)
        top = jnp.where(upper, value, zero)
        low = jnp.where(upper, zero, value)
        own[ri] = jnp.where(left, top, zero)
        right[ri] = jnp.where(left, zero, top).astype(BF16)
        below[ri] = jnp.where(left, low, zero).astype(BF16)
        corner[ri] = jnp.where(left, zero, low).astype(BF16)


def scan_sum_kernel(ids, src, out, total):
    total[...] = jnp.zeros_like(total)
    for d in range(NYLX * NYH):
        s = ids[d]
        total[s] += src[d].astype(F32)
    for s in range(SCANS):
        out[:, s] = total[s].astype(BF16)


def shape(dims, dtype):
    return jax.ShapeDtypeStruct(dims, dtype)


def whole(kernel, out_shape, scalars, arrays, scratch=()):
    spec = pl.BlockSpec(memory_space=VMEM)
    single = not isinstance(out_shape, (list, tuple))
    return pl.pallas_call(
        kernel,
        grid_spec=pltpu.PrefetchScalarGridSpec(
            num_scalar_prefetch=1,
            grid=(),
            in_specs=[spec] * len(arrays),
            out_specs=spec if single else [spec] * len(out_shape),
            scratch_shapes=list(scratch),
        ),
        out_shape=out_shape,
    )(scalars, *arrays)


def fixed(dims):
    return pl.BlockSpec(dims, lambda g, info: (0,) * len(dims))


def stepped(dims, axis):
    return pl.BlockSpec(dims, lambda g, info: tuple(g if a == axis else 0 for a in range(len(dims))))


PAIR = (2, 2, W, W)
BLOCKS = (NYLX, 1, NZ, 16, W)
ALL_BLOCKS = (NYLX, NYH, NZ, 16, W)


def forward(info, blocks, mine, other, consts):
    plus, minus, kern, order = consts
    half = (2, W, W)
    return pl.pallas_call(
        forward_kernel,
        grid_spec=pltpu.PrefetchScalarGridSpec(
            num_scalar_prefetch=1,
            grid=(2,),
            in_specs=[
                stepped(BLOCKS, 1),
                fixed(half),
                fixed(half),
                fixed((2 * W, 2 * W)),
                fixed((2 * W, 2 * W)),
                fixed(half),
                fixed((128, 128)),
            ],
            out_specs=[stepped(PAIR, 0), stepped(PAIR, 0), stepped(PAIR, 0), fixed((W, W))],
        ),
        out_shape=[shape((4, 2, W, W), BF16)] * 3 + [shape((W, W), F32)],
        compiler_params=pltpu.CompilerParams(dimension_semantics=("arbitrary",)),
    )(info, blocks, mine, other, plus, minus, kern, order)


def backward(info, psi, inc, far, power_a, power_b, patterns, mine, other, consts):
    plus, minus, kern, order = consts
    half = (2, W, W)
    return pl.pallas_call(
        backward_kernel,
        grid_spec=pltpu.PrefetchScalarGridSpec(
            num_scalar_prefetch=1,
            grid=(2,),
            in_specs=[
                stepped(PAIR, 0),
                stepped(PAIR, 0),
                stepped(PAIR, 0),
                fixed((W, W)),
                fixed((W, W)),
                pl.BlockSpec((1, W, W), lambda g, info: (info[3], 0, 0)),
                fixed(half),
                fixed(half),
                fixed((2 * W, 2 * W)),
                fixed((2 * W, 2 * W)),
                fixed(half),
                fixed((128, 128)),
            ],
            out_specs=[fixed(PAIR), stepped(BLOCKS, 1)],
            scratch_shapes=[VMEM(PAIR, BF16)],
        ),
        out_shape=[shape(PAIR, F32), shape(ALL_BLOCKS, BF16)],
        compiler_params=pltpu.CompilerParams(dimension_semantics=("arbitrary",)),
    )(info, psi, inc, far, power_a, power_b, patterns, mine, other, plus, minus, kern, order)


def swap(value, axis):
    return lax.ppermute(value, axis, [(0, 1), (1, 0)])


def from_tile(value, distance):
    route = [(t + distance, t) for t in range(TILES) if 0 <= t + distance < TILES]
    return lax.ppermute(value, TILE_AXES, route)


def exchange(value, axes):
    return lax.all_to_all(value, axes, 0, 0, tiled=True)


def spread(value, axes, count):
    return exchange(jnp.broadcast_to(value[None], (count,) + value.shape), axes)


def body(
    object_tiles,
    object_previous,
    probe,
    probe_previous,
    patterns,
    offsets,
    scan_of_slot,
    tile_load,
    step_sizes,
    object_norm_before,
    probe_norm_before,
):
    core = lax.axis_index("c")
    slot = lax.axis_index("yh")
    plus, minus, kern, order = tables()
    consts = (
        jnp.asarray(plus, BF16),
        jnp.asarray(minus, BF16),
        jnp.asarray(kern, F32),
        jnp.asarray(order, BF16),
    )
    my_offset = lax.dynamic_index_in_dim(offsets, slot, 1, keepdims=False)
    used = (slot < tile_load[0]).astype(jnp.int32)
    info = jnp.stack([my_offset[0], my_offset[1], core.astype(jnp.int32), slot.astype(jnp.int32), used])

    with jax.named_scope("ids"):
        id_row = jnp.broadcast_to(jnp.pad(scan_of_slot, (0, 126))[None, :], (8, 128))
        ids = spread(id_row, ("yl", "x"), NYLX)[:, 0, :2].reshape(NYLX * NYH)

    with jax.named_scope("object_in"):
        own = lax.dynamic_index_in_dim(object_tiles[0], core, 0, keepdims=False).astype(BF16)
        east, south, corner = (from_tile(own, d) for d in (1, TGX, TGX + 1))

    with jax.named_scope("probe_z"):
        rows = probe.astype(BF16).reshape(SCANS * 16, W)
        banded = spread(rows, "z", NZ).reshape(NZ, SCANS, 16, W)
    with jax.named_scope("probe_plane"):
        picked = whole(pick_kernel, shape((NYLX * NYH, NZ, 16, W), BF16), ids, [banded])
        blocks = exchange(picked, PLANE).reshape(ALL_BLOCKS)

    with jax.named_scope("patch"):
        mine = whole(patch_kernel, shape((2, W, W), BF16), info, [own, east, south, corner])
        other = swap(mine, "c")

    psi, inc, far, power = forward(info, blocks, mine, other, consts)
    with jax.named_scope("power"):
        power_other = swap(power, "c")
    terms, probe_terms = backward(info, psi, inc, far, power, power_other, patterns, mine, other, consts)

    with jax.named_scope("object_core"):
        theirs = swap(terms[1].astype(BF16), "c")
    with jax.named_scope("place"):
        half = (2, W, W)
        kept, right, below, diagonal = whole(
            place_kernel, [shape(half, F32)] + [shape(half, BF16)] * 3, info, [terms[0], theirs]
        )
    with jax.named_scope("object_out"):
        from_left, from_above, from_corner = (
            from_tile(v, -d) for v, d in ((right, 1), (below, TGX), (diagonal, TGX + 1))
        )
    with jax.named_scope("grad_plane"):
        received = exchange(probe_terms.reshape(NYLX * NYH, NZ, 16, W), PLANE)
        by_scan = whole(
            scan_sum_kernel,
            shape((NZ, SCANS, 16, W), BF16),
            ids,
            [received],
            [VMEM((SCANS, NZ, 16, W), F32)],
        )
    with jax.named_scope("object_slots"):
        layer_part = (
            kept + from_left.astype(F32) + from_above.astype(F32) + from_corner.astype(F32)
        ).astype(BF16)
        layer_grad = layer_part.astype(F32) + swap(layer_part, "yh").astype(F32)
    with jax.named_scope("object_layers"):
        other_grad = swap(layer_grad, "c")
        first = core == 0
        tile_grad = jnp.stack(
            [jnp.where(first, layer_grad, other_grad), jnp.where(first, other_grad, layer_grad)]
        )
    with jax.named_scope("grad_z"):
        summed = exchange(by_scan.reshape(NZ, SCANS * 16, W), "z")
        probe_grad = jnp.sum(summed.astype(F32), axis=0).reshape(SCANS, 2, 2, ROWS, W)

    with jax.named_scope("norms"):
        object_part = jnp.sum(tile_grad * tile_grad)
        probe_part = jnp.sum(probe_grad * probe_grad)
        probe_part = probe_part + swap(probe_part.reshape(1), "c")[0]
        lane = lax.broadcasted_iota(jnp.int32, (8, 128), 1)
        packed = jnp.where(lane == 0, object_part, probe_part)
        packed = jnp.sum(spread(packed, PLANE, NYLX * NYH), axis=0)
        packed = jnp.sum(spread(packed, "z", NZ), axis=0)
        object_square = packed[0, 0] / float(NYH * TILES * LAYERS * 2 * W * W)
        probe_square = packed[0, 1] / float(SCANS * MODES * 2 * W * W)

    object_direction = -tile_grad[None] + object_square / object_norm_before[0] * object_previous
    new_object = object_tiles + step_sizes[0].astype(F32) / 1024.0 * object_direction
    probe_direction = -probe_grad + probe_square / probe_norm_before[0] * probe_previous
    new_probe = probe + step_sizes[1].astype(F32) / 16384.0 * probe_direction
    return (new_object, object_direction, new_probe, probe_direction)


def solution(mesh):
    fine = Mesh(mesh.devices.reshape(NZ, NYL, NX, NYH, NC), ("z", "yl", "x", "yh", "c"))
    tile, mode = TILE_AXES, ("yh", "c")
    objects = P(tile, None, None, None, None)
    probes = P(None, mode, None, tile, None)
    return jax.shard_map(
        body,
        mesh=fine,
        in_specs=(
            objects,
            objects,
            probes,
            probes,
            P(tile, None, None),
            P(None, tile),
            P(tile),
            P(tile),
            P(),
            P(),
            P(),
        ),
        out_specs=(objects, objects, probes, probes),
        check_vma=False,
    )
```

```python
import math

import jax
import jax.numpy as jnp
import numpy as np
from jax import lax
from jax.experimental import pallas as pl
from jax.experimental.pallas import tpu as pltpu
from jax.sharding import Mesh, PartitionSpec as P

TGX = 8
LAYERS = 2
MODES = 8
SCANS = 4
W = 256
NZ, NYL, NX, NYH, NC = 8, 2, 4, 2, 2
NYLX = NYL * NX
TILES = NZ * NYLX
ROWS = W // TILES
BAND = NYLX * ROWS
TILE_AXES = ("z", "yl", "x")
PLANE = ("yl", "x", "yh")
VMEM = pltpu.VMEM
F32 = jnp.float32
BF16 = jnp.bfloat16


def tables():
    index = np.arange(W, dtype=np.int64)
    angle = ((index[:, None] * index[None, :]) % W).astype(np.float32) * np.float32(2.0 * math.pi / W)
    factor = np.float32(1.0 / math.sqrt(W))
    cosine = np.cos(angle, dtype=np.float32) * factor
    sine = -np.sin(angle, dtype=np.float32) * factor
    plus = np.block([[cosine, sine], [-sine, cosine]])
    minus = np.block([[cosine, -sine], [sine, cosine]])
    free = np.where(index < W // 2, index, index - W).astype(np.float32)
    phase = (free[:, None] * free[:, None] + free[None, :] * free[None, :]) * np.float32(math.pi / (4.0 * W))
    kernel = np.stack([np.cos(phase, dtype=np.float32), np.sin(phase, dtype=np.float32)])
    rows = np.arange(128)
    band, i, ri, r = rows // 16, rows // 8 % 2, rows // 4 % 2, rows % 4
    natural = i * 64 + ri * 32 + band * 4 + r
    order = np.zeros((128, 128), np.float32)
    order[natural, rows] = 1.0
    return plus, minus, kernel, order


def mm(a, b):
    return jnp.dot(a, b, preferred_element_type=F32)


def transform(wave_re, wave_im, right, left):
    across = jnp.concatenate([wave_re, wave_im], axis=1)
    first = mm(across, right).astype(BF16)
    down = jnp.concatenate([first[:, :W], first[:, W:]], axis=0)
    out = mm(left, down).astype(BF16)
    return out[:W], out[W:]


def times(a_re, a_im, b_re, b_im):
    a_re, a_im, b_re, b_im = (v.astype(F32) for v in (a_re, a_im, b_re, b_im))
    return a_re * b_re - a_im * b_im, a_re * b_im + a_im * b_re


def conj_times(a_re, a_im, b_re, b_im):
    a_re, a_im, b_re, b_im = (v.astype(F32) for v in (a_re, a_im, b_re, b_im))
    return a_re * b_re + a_im * b_im, a_re * b_im - a_im * b_re


def window_masks(row, col):
    rows = lax.broadcasted_iota(jnp.int32, (W, W), 0)
    cols = lax.broadcasted_iota(jnp.int32, (W, W), 1)
    return rows >= row, cols >= col


def patch_kernel(info, own, east, low, out):
    row, col = info[0], info[1]
    upper, left = window_masks(row, col)
    for ri in range(2):
        top = jnp.where(left, own[ri].astype(F32), east[ri].astype(F32))
        value = jnp.where(upper, top, low[ri].astype(F32))
        value = pltpu.roll(value, (W - row) % W, 0)
        value = pltpu.roll(value, (W - col) % W, 1)
        out[ri] = value.astype(BF16)


def pick_kernel(ids, src, out):
    for d in range(NYLX * NYH):
        out[d] = src[:, ids[d]]


def forward_kernel(info, blocks, mine, other, plus, minus, kern, order, psi, inc, far, power):
    step = pl.program_id(0)
    first = info[2] == 0
    for z in range(NZ):
        piece = blocks[:, 0, z].reshape(128, W)
        placed = mm(order[...], piece).astype(BF16)
        for i in range(2):
            for ri in range(2):
                at = i * 64 + ri * 32
                psi[i, ri, z * BAND : (z + 1) * BAND] = placed[at : at + BAND]
    fwd, inv = plus[...], minus[...]
    p0 = [jnp.where(first, mine[ri], other[ri]) for ri in range(2)]
    p1 = [jnp.where(first, other[ri], mine[ri]) for ri in range(2)]
    total = None
    for i in range(2):
        e_re, e_im = times(psi[i, 0], psi[i, 1], p0[0], p0[1])
        s_re, s_im = transform(e_re.astype(BF16), e_im.astype(BF16), fwd, inv)
        m_re, m_im = times(s_re, s_im, kern[0], kern[1])
        w_re, w_im = transform(m_re.astype(BF16), m_im.astype(BF16), inv, fwd)
        inc[i, 0] = w_re
        inc[i, 1] = w_im
        e_re, e_im = times(w_re, w_im, p1[0], p1[1])
        f_re, f_im = transform(e_re.astype(BF16), e_im.astype(BF16), fwd, inv)
        far[i, 0] = f_re
        far[i, 1] = f_im
        f_re, f_im = f_re.astype(F32), f_im.astype(F32)
        part = f_re * f_re + f_im * f_im
        total = part if total is None else total + part

    @pl.when(step == 0)
    def _():
        power[...] = total

    @pl.when(step != 0)
    def _():
        power[...] += total


def backward_kernel(
    info, psi, inc, far, power_a, power_b, pattern, mine, other, plus, minus, kern, order, terms, out, scratch
):
    step = pl.program_id(0)
    core = info[2]
    first = core == 0
    used = info[4].astype(F32)
    fwd, inv = plus[...], minus[...]
    p0 = [jnp.where(first, mine[ri], other[ri]) for ri in range(2)]
    p1 = [jnp.where(first, other[ri], mine[ri]) for ri in range(2)]
    double = 2.0 * ((power_a[...] + power_b[...] - pattern[0]) * used)
    sums = [None] * 4
    for i in range(2):
        b_re = (double * far[i, 0].astype(F32)).astype(BF16)
        b_im = (double * far[i, 1].astype(F32)).astype(BF16)
        b_re, b_im = transform(b_re, b_im, inv, fwd)
        t1 = conj_times(inc[i, 0], inc[i, 1], b_re, b_im)
        c_re, c_im = conj_times(p1[0], p1[1], b_re, b_im)
        s_re, s_im = transform(c_re.astype(BF16), c_im.astype(BF16), fwd, inv)
        m_re, m_im = times(s_re, s_im, kern[0], -kern[1])
        b_re, b_im = transform(m_re.astype(BF16), m_im.astype(BF16), inv, fwd)
        t0 = conj_times(psi[i, 0], psi[i, 1], b_re, b_im)
        c_re, c_im = conj_times(p0[0], p0[1], b_re, b_im)
        scratch[i, 0] = c_re.astype(BF16)
        scratch[i, 1] = c_im.astype(BF16)
        new = [t0[0], t0[1], t1[0], t1[1]]
        sums = [n if s is None else s + n for s, n in zip(sums, new)]
    back = order[...].T
    for z in range(NZ):
        pieces = [
            scratch[i, ri, z * BAND : (z + 1) * BAND] for i in range(2) for ri in range(2)
        ]
        piece = mm(back, jnp.concatenate(pieces, axis=0)).astype(BF16)
        out[:, 0, z] = piece.reshape(NYLX, 16, W)
    for layer in range(LAYERS):
        slot = core if layer == 0 else 1 - core

        @pl.when(step == 0)
        def _():
            terms[slot, 0] = sums[2 * layer]
            terms[slot, 1] = sums[2 * layer + 1]

        @pl.when(step != 0)
        def _():
            terms[slot, 0] += sums[2 * layer]
            terms[slot, 1] += sums[2 * layer + 1]


def place_kernel(info, mine, theirs, up, low):
    row, col = info[0], info[1]
    upper, _ = window_masks(row, col)
    zero = jnp.zeros((W, W), F32)
    for ri in range(2):
        value = mine[ri] + theirs[ri].astype(F32)
        value = pltpu.roll(value, row, 0)
        value = pltpu.roll(value, col, 1)
        up[ri] = jnp.where(upper, value, zero)
        low[ri] = jnp.where(upper, zero, value).astype(BF16)


def scan_sum_kernel(ids, src, out, total):
    total[...] = jnp.zeros_like(total)
    for d in range(NYLX * NYH):
        s = ids[d]
        total[s] += src[d].astype(F32)
    for s in range(SCANS):
        out[:, s] = total[s].astype(BF16)


def shape(dims, dtype):
    return jax.ShapeDtypeStruct(dims, dtype)


def whole(kernel, out_shape, scalars, arrays, scratch=()):
    spec = pl.BlockSpec(memory_space=VMEM)
    single = not isinstance(out_shape, (list, tuple))
    return pl.pallas_call(
        kernel,
        grid_spec=pltpu.PrefetchScalarGridSpec(
            num_scalar_prefetch=1,
            grid=(),
            in_specs=[spec] * len(arrays),
            out_specs=spec if single else [spec] * len(out_shape),
            scratch_shapes=list(scratch),
        ),
        out_shape=out_shape,
        compiler_params=pltpu.CompilerParams(vmem_limit_bytes=8 << 20),
    )(scalars, *arrays)


def fixed(dims):
    return pl.BlockSpec(dims, lambda g, info: (0,) * len(dims))


def stepped(dims, axis):
    return pl.BlockSpec(dims, lambda g, info: tuple(g if a == axis else 0 for a in range(len(dims))))


PAIR = (2, 2, W, W)
BLOCKS = (NYLX, 1, NZ, 16, W)
ALL_BLOCKS = (NYLX, NYH, NZ, 16, W)


def forward(info, blocks, mine, other, consts):
    plus, minus, kern, order = consts
    half = (2, W, W)
    return pl.pallas_call(
        forward_kernel,
        grid_spec=pltpu.PrefetchScalarGridSpec(
            num_scalar_prefetch=1,
            grid=(2,),
            in_specs=[
                stepped(BLOCKS, 1),
                fixed(half),
                fixed(half),
                fixed((2 * W, 2 * W)),
                fixed((2 * W, 2 * W)),
                fixed(half),
                fixed((128, 128)),
            ],
            out_specs=[stepped(PAIR, 0), stepped(PAIR, 0), stepped(PAIR, 0), fixed((W, W))],
        ),
        out_shape=[shape((4, 2, W, W), BF16)] * 3 + [shape((W, W), F32)],
        compiler_params=pltpu.CompilerParams(dimension_semantics=("arbitrary",), vmem_limit_bytes=28 << 20),
    )(info, blocks, mine, other, plus, minus, kern, order)


def backward(info, psi, inc, far, power_a, power_b, patterns, mine, other, consts):
    plus, minus, kern, order = consts
    half = (2, W, W)
    return pl.pallas_call(
        backward_kernel,
        grid_spec=pltpu.PrefetchScalarGridSpec(
            num_scalar_prefetch=1,
            grid=(2,),
            in_specs=[
                stepped(PAIR, 0),
                stepped(PAIR, 0),
                stepped(PAIR, 0),
                fixed((W, W)),
                fixed((W, W)),
                pl.BlockSpec((1, W, W), lambda g, info: (info[3], 0, 0)),
                fixed(half),
                fixed(half),
                fixed((2 * W, 2 * W)),
                fixed((2 * W, 2 * W)),
                fixed(half),
                fixed((128, 128)),
            ],
            out_specs=[fixed(PAIR), stepped(BLOCKS, 1)],
            scratch_shapes=[VMEM(PAIR, BF16)],
        ),
        out_shape=[shape(PAIR, F32), shape(ALL_BLOCKS, BF16)],
        compiler_params=pltpu.CompilerParams(dimension_semantics=("arbitrary",), vmem_limit_bytes=28 << 20),
    )(info, psi, inc, far, power_a, power_b, patterns, mine, other, plus, minus, kern, order)


def swap(value, axis):
    return lax.ppermute(value, axis, [(0, 1), (1, 0)])


def from_tile(value, distance):
    route = [(t + distance, t) for t in range(TILES) if 0 <= t + distance < TILES]
    return lax.ppermute(value, TILE_AXES, route)


def exchange(value, axes):
    return lax.all_to_all(value, axes, 0, 0, tiled=True)


def spread(value, axes, count):
    return exchange(jnp.broadcast_to(value[None], (count,) + value.shape), axes)


def update(
    object_tiles,
    object_previous,
    probe,
    probe_previous,
    patterns,
    offsets,
    scan_of_slot,
    tile_load,
    step_sizes,
    object_norm_before,
    probe_norm_before,
):
    core = lax.axis_index("c")
    slot = lax.axis_index("yh")
    plus, minus, kern, order = tables()
    consts = (
        jnp.asarray(plus, BF16),
        jnp.asarray(minus, BF16),
        jnp.asarray(kern, F32),
        jnp.asarray(order, BF16),
    )
    my_offset = lax.dynamic_index_in_dim(offsets, slot, 1, keepdims=False)
    used = (slot < tile_load[0]).astype(jnp.int32)
    info = jnp.stack([my_offset[0], my_offset[1], core.astype(jnp.int32), slot.astype(jnp.int32), used])
    columns = lax.broadcasted_iota(jnp.int32, (1, 1, W), 2)
    my_left = columns >= my_offset[1]

    at = lax.broadcasted_iota(jnp.int32, (1, 128), 1)
    here = 2 * (NX * lax.axis_index("yl") + lax.axis_index("x"))
    row = jnp.where(at == here, scan_of_slot[0], 0) + jnp.where(at == here + 1, scan_of_slot[1], 0)
    rows = [row]
    for d in range(1, NX):
        rows.append(lax.ppermute(row, "x", [((x + d) % NX, x) for x in range(NX)]))
    row = sum(rows[1:], rows[0])
    row = row + swap(row, "yl")
    ids = row[0, : NYLX * NYH]

    own = lax.dynamic_index_in_dim(object_tiles[0], core, 0, keepdims=False).astype(BF16)
    col_row = jnp.broadcast_to(my_offset[1].reshape(1, 1), (1, 128))
    above_col = from_tile(col_row, -TGX)[:1, :1].reshape(1, 1, 1)
    above_left = columns >= above_col
    east = from_tile(own, 1)
    south = from_tile(jnp.where(above_left, own, east), TGX)

    rows = probe.astype(BF16).reshape(SCANS * 16, W)
    banded = spread(rows, "z", NZ).reshape(NZ, SCANS, 16, W)
    picked = whole(pick_kernel, shape((NYLX * NYH, NZ, 16, W), BF16), ids, [banded])
    blocks = exchange(picked, PLANE).reshape(ALL_BLOCKS)

    mine = whole(patch_kernel, shape((2, W, W), BF16), info, [own, east, south])
    other = swap(mine, "c")

    psi, inc, far, power = forward(info, blocks, mine, other, consts)
    power_other = swap(power, "c")
    terms, probe_terms = backward(info, psi, inc, far, power, power_other, patterns, mine, other, consts)

    theirs = swap(terms[1].astype(BF16), "c")
    half = (2, W, W)
    up, low = whole(place_kernel, [shape(half, F32), shape(half, BF16)], info, [terms[0], theirs])
    from_above = from_tile(low, -TGX).astype(F32)
    kept = jnp.where(my_left, up, 0.0) + jnp.where(above_left, from_above, 0.0)
    right = jnp.where(my_left, 0.0, up) + jnp.where(above_left, 0.0, from_above)
    from_left = from_tile(right.astype(BF16), -1)
    received = exchange(probe_terms.reshape(NYLX * NYH, NZ, 16, W), PLANE)
    by_scan = whole(scan_sum_kernel, shape((NZ, SCANS, 16, W), BF16), ids, [received], [VMEM((SCANS, NZ, 16, W), F32)])
    layer_part = (kept + from_left.astype(F32)).astype(BF16)
    layer_grad = layer_part.astype(F32) + swap(layer_part, "yh").astype(F32)
    other_grad = swap(layer_grad, "c")
    first = core == 0
    tile_grad = jnp.stack(
        [jnp.where(first, layer_grad, other_grad), jnp.where(first, other_grad, layer_grad)]
    )
    summed = exchange(by_scan.reshape(NZ, SCANS * 16, W), "z")
    probe_grad = jnp.sum(summed.astype(F32), axis=0).reshape(SCANS, 2, 2, ROWS, W)

    lane = lax.broadcasted_iota(jnp.int32, (1, 128), 1)
    object_part = jnp.sum(layer_grad * layer_grad)
    probe_part = jnp.sum(probe_grad * probe_grad)
    packed = jnp.where(lane == 0, object_part, probe_part)
    packed = packed + swap(packed, "c")
    packed = jnp.sum(spread(packed, ("z",) + PLANE, TILES * NYH), axis=0)
    object_square = packed[0, 0] / float(NYH * TILES * LAYERS * 2 * W * W)
    probe_square = packed[0, 1] / float(SCANS * MODES * 2 * W * W)

    object_direction = -tile_grad[None] + object_square / object_norm_before[0] * object_previous
    new_object = object_tiles + step_sizes[0].astype(F32) / 1024.0 * object_direction
    probe_direction = -probe_grad + probe_square / probe_norm_before[0] * probe_previous
    new_probe = probe + step_sizes[1].astype(F32) / 16384.0 * probe_direction
    return (new_object, object_direction, new_probe, probe_direction)


def solution(mesh):
    fine = Mesh(mesh.devices.reshape(NZ, NYL, NX, NYH, NC), ("z", "yl", "x", "yh", "c"))
    tile, mode = TILE_AXES, ("yh", "c")
    objects = P(tile, None, None, None, None)
    probes = P(None, mode, None, tile, None)
    return jax.shard_map(
        update,
        mesh=fine,
        in_specs=(
            objects,
            objects,
            probes,
            probes,
            P(tile, None, None),
            P(None, tile),
            P(tile),
            P(tile),
            P(),
            P(),
            P(),
        ),
        out_specs=(objects, objects, probes, probes),
        check_vma=False,
    )
```

```python
import math

import jax
import jax.numpy as jnp
import numpy as np
from jax import lax
from jax.experimental import pallas as pl
from jax.experimental.pallas import tpu as pltpu
from jax.sharding import Mesh, PartitionSpec as P

TGX = 8
LAYERS = 2
MODES = 8
SCANS = 4
W = 256
NZ, NYL, NX, NYH, NC = 8, 2, 4, 2, 2
NYLX = NYL * NX
TILES = NZ * NYLX
ROWS = W // TILES
BAND = NYLX * ROWS
TILE_AXES = ("z", "yl", "x")
PLANE = ("yl", "x", "yh")
VMEM = pltpu.VMEM
F32 = jnp.float32
BF16 = jnp.bfloat16


def tables():
    index = np.arange(W, dtype=np.int64)
    angle = ((index[:, None] * index[None, :]) % W).astype(np.float32) * np.float32(2.0 * math.pi / W)
    factor = np.float32(1.0 / math.sqrt(W))
    cosine = np.cos(angle, dtype=np.float32) * factor
    sine = -np.sin(angle, dtype=np.float32) * factor
    dft = np.stack([cosine, sine])
    free = np.where(index < W // 2, index, index - W).astype(np.float32)
    phase = (free[:, None] * free[:, None] + free[None, :] * free[None, :]) * np.float32(math.pi / (4.0 * W))
    kernel = np.stack([np.cos(phase, dtype=np.float32), np.sin(phase, dtype=np.float32)])
    rows = np.arange(128)
    band, i, ri, r = rows // 16, rows // 8 % 2, rows // 4 % 2, rows % 4
    natural = i * 64 + ri * 32 + band * 4 + r
    order = np.zeros((128, 128), np.float32)
    order[natural, rows] = 1.0
    return dft, kernel, order


def mm(a, b):
    return jnp.dot(a, b, preferred_element_type=F32)


def transform(pairs, right, left):
    across = jnp.concatenate([jnp.concatenate(p, axis=1) for p in pairs], axis=0)
    first = mm(across.astype(BF16), right).astype(BF16)
    spans = [slice(i * W, (i + 1) * W) for i in range(len(pairs))]
    down = jnp.concatenate(
        [
            jnp.concatenate([first[at, :W] for at in spans], axis=1),
            jnp.concatenate([first[at, W:] for at in spans], axis=1),
        ],
        axis=0,
    )
    out = mm(left, down).astype(BF16)
    return [(out[:W, at], out[W:, at]) for at in spans]


def times(a_re, a_im, b_re, b_im):
    a_re, a_im, b_re, b_im = (v.astype(F32) for v in (a_re, a_im, b_re, b_im))
    return a_re * b_re - a_im * b_im, a_re * b_im + a_im * b_re


def conj_times(a_re, a_im, b_re, b_im):
    a_re, a_im, b_re, b_im = (v.astype(F32) for v in (a_re, a_im, b_re, b_im))
    return a_re * b_re + a_im * b_im, a_re * b_im - a_im * b_re


def fill(step, dft, plus, minus):
    @pl.when(step == 0)
    def _():
        for i in range(2):
            at = slice(i * W, (i + 1) * W)
            plus[at, at] = dft[0]
            minus[at, at] = dft[0]
        for ref, a, b in ((plus, dft[1], -dft[1]), (minus, -dft[1], dft[1])):
            ref[:W, W:] = a
            ref[W:, :W] = b


def window_masks(row, col):
    rows = lax.broadcasted_iota(jnp.int32, (W, W), 0)
    cols = lax.broadcasted_iota(jnp.int32, (W, W), 1)
    return rows >= row, cols >= col


def patch_kernel(info, own, east, low, out):
    row, col = info[0], info[1]
    upper, left = window_masks(row, col)
    for ri in range(2):
        top = jnp.where(left, own[ri].astype(F32), east[ri].astype(F32))
        value = jnp.where(upper, top, low[ri].astype(F32))
        value = pltpu.roll(value, (W - row) % W, 0)
        value = pltpu.roll(value, (W - col) % W, 1)
        out[ri] = value.astype(BF16)


def pick_kernel(ids, src, out):
    for d in range(NYLX * NYH):
        out[d] = src[:, ids[d]]


def forward_kernel(info, blocks, mine, other, dft, kern, order, psi, inc, far, power, plus, minus):
    step = pl.program_id(0)
    first = info[2] == 0
    fill(step, dft, plus, minus)
    for z in range(NZ):
        piece = blocks[:, 0, z].reshape(128, W)
        placed = mm(order[...], piece).astype(BF16)
        for i in range(2):
            for ri in range(2):
                at = i * 64 + ri * 32
                psi[i, ri, z * BAND : (z + 1) * BAND] = placed[at : at + BAND]
    fwd, inv = plus[...], minus[...]
    p0 = [jnp.where(first, mine[ri], other[ri]) for ri in range(2)]
    p1 = [jnp.where(first, other[ri], mine[ri]) for ri in range(2)]
    pairs = range(2)
    spec = transform([times(psi[i, 0], psi[i, 1], *p0) for i in pairs], fwd, inv)
    moved = transform([times(*spec[i], kern[0], kern[1]) for i in pairs], inv, fwd)
    for i in pairs:
        inc[i, 0], inc[i, 1] = moved[i]
    waves = transform([times(*moved[i], *p1) for i in pairs], fwd, inv)
    total = None
    for i in pairs:
        far[i, 0], far[i, 1] = waves[i]
        f_re, f_im = waves[i][0].astype(F32), waves[i][1].astype(F32)
        part = f_re * f_re + f_im * f_im
        total = part if total is None else total + part

    @pl.when(step == 0)
    def _():
        power[...] = total

    @pl.when(step != 0)
    def _():
        power[...] += total


def backward_kernel(
    info, psi, inc, far, power_a, power_b, pattern, mine, other, dft, kern, order, terms, out, scratch, plus, minus
):
    step = pl.program_id(0)
    core = info[2]
    first = core == 0
    fill(step, dft, plus, minus)
    used = info[4].astype(F32)
    fwd, inv = plus[...], minus[...]
    p0 = [jnp.where(first, mine[ri], other[ri]) for ri in range(2)]
    p1 = [jnp.where(first, other[ri], mine[ri]) for ri in range(2)]
    double = 2.0 * ((power_a[...] + power_b[...] - pattern[0]) * used)
    pairs = range(2)
    back = transform([[double * far[i, ri].astype(F32) for ri in range(2)] for i in pairs], inv, fwd)
    term1 = [conj_times(inc[i, 0], inc[i, 1], *back[i]) for i in pairs]
    spec = transform([conj_times(*p1, *back[i]) for i in pairs], fwd, inv)
    back = transform([times(*spec[i], kern[0], -kern[1]) for i in pairs], inv, fwd)
    term0 = [conj_times(psi[i, 0], psi[i, 1], *back[i]) for i in pairs]
    for i in pairs:
        for ri, value in enumerate(conj_times(*p0, *back[i])):
            scratch[i, ri] = value.astype(BF16)
    sums = [t[0][ri] + t[1][ri] for t in (term0, term1) for ri in range(2)]
    back = order[...].T
    for z in range(NZ):
        pieces = [
            scratch[i, ri, z * BAND : (z + 1) * BAND] for i in range(2) for ri in range(2)
        ]
        piece = mm(back, jnp.concatenate(pieces, axis=0)).astype(BF16)
        out[:, 0, z] = piece.reshape(NYLX, 16, W)
    for layer in range(LAYERS):
        slot = core if layer == 0 else 1 - core

        @pl.when(step == 0)
        def _():
            terms[slot, 0] = sums[2 * layer]
            terms[slot, 1] = sums[2 * layer + 1]

        @pl.when(step != 0)
        def _():
            terms[slot, 0] += sums[2 * layer]
            terms[slot, 1] += sums[2 * layer + 1]


def place_kernel(info, mine, theirs, up, low):
    row, col = info[0], info[1]
    upper, _ = window_masks(row, col)
    zero = jnp.zeros((W, W), F32)
    for ri in range(2):
        value = mine[ri] + theirs[ri].astype(F32)
        value = pltpu.roll(value, row, 0)
        value = pltpu.roll(value, col, 1)
        up[ri] = jnp.where(upper, value, zero)
        low[ri] = jnp.where(upper, zero, value).astype(BF16)


def scan_sum_kernel(src, ids, out):
    wide = NYLX * NYH * 16
    spread_of = lax.broadcasted_iota(jnp.int32, (128, wide), 1) // 16
    expand = (spread_of == lax.broadcasted_iota(jnp.int32, (128, wide), 0)).astype(BF16)
    idrow = jnp.broadcast_to(ids[...], (8, 128)).astype(F32).astype(BF16)
    scan = mm(idrow, expand)[:1]
    target = lax.broadcasted_iota(jnp.int32, (SCANS * 16, wide), 0)
    column = lax.broadcasted_iota(jnp.int32, (SCANS * 16, wide), 1)
    take = (scan == (target // 16).astype(F32)) & (target % 16 == column % 16)
    take = take.astype(BF16)
    for z in range(NZ):
        out[z] = mm(take, src[:, z].reshape(wide, W)).astype(BF16)


def grad_sum_kernel(src, layer, out, packed):
    total = src[0].astype(F32)
    for z in range(1, NZ):
        total += src[z].astype(F32)
    out[...] = total
    object_part = jnp.sum(layer[...] * layer[...])
    probe_part = jnp.sum(total * total)
    lane = lax.broadcasted_iota(jnp.int32, (1, 128), 1)
    packed[...] = jnp.where(lane == 0, object_part, probe_part)


def plain(kernel, out_shape, *arrays):
    spec = pl.BlockSpec(memory_space=VMEM)
    single = not isinstance(out_shape, (list, tuple))
    return pl.pallas_call(
        kernel,
        in_specs=[spec] * len(arrays),
        out_specs=spec if single else [spec] * len(out_shape),
        out_shape=out_shape,
        compiler_params=pltpu.CompilerParams(vmem_limit_bytes=8 << 20),
    )(*arrays)


def shape(dims, dtype):
    return jax.ShapeDtypeStruct(dims, dtype)


def whole(kernel, out_shape, scalars, arrays, scratch=()):
    spec = pl.BlockSpec(memory_space=VMEM)
    single = not isinstance(out_shape, (list, tuple))
    return pl.pallas_call(
        kernel,
        grid_spec=pltpu.PrefetchScalarGridSpec(
            num_scalar_prefetch=1,
            grid=(),
            in_specs=[spec] * len(arrays),
            out_specs=spec if single else [spec] * len(out_shape),
            scratch_shapes=list(scratch),
        ),
        out_shape=out_shape,
        compiler_params=pltpu.CompilerParams(vmem_limit_bytes=8 << 20),
    )(scalars, *arrays)


def fixed(dims):
    return pl.BlockSpec(dims, lambda g, info: (0,) * len(dims))


def stepped(dims, axis):
    return pl.BlockSpec(dims, lambda g, info: tuple(g if a == axis else 0 for a in range(len(dims))))


PAIR = (2, 2, W, W)
BLOCKS = (NYLX, 1, NZ, 16, W)
ALL_BLOCKS = (NYLX, NYH, NZ, 16, W)


def forward(info, blocks, mine, other, consts):
    dft, kern, order = consts
    half = (2, W, W)
    return pl.pallas_call(
        forward_kernel,
        grid_spec=pltpu.PrefetchScalarGridSpec(
            num_scalar_prefetch=1,
            grid=(2,),
            in_specs=[
                stepped(BLOCKS, 1),
                fixed(half),
                fixed(half),
                fixed(half),
                fixed(half),
                fixed((128, 128)),
            ],
            out_specs=[stepped(PAIR, 0), stepped(PAIR, 0), stepped(PAIR, 0), fixed((W, W))],
            scratch_shapes=[VMEM((2 * W, 2 * W), BF16), VMEM((2 * W, 2 * W), BF16)],
        ),
        out_shape=[shape((4, 2, W, W), BF16)] * 3 + [shape((W, W), F32)],
        compiler_params=pltpu.CompilerParams(dimension_semantics=("arbitrary",), vmem_limit_bytes=28 << 20),
    )(info, blocks, mine, other, dft, kern, order)


def backward(info, psi, inc, far, power_a, power_b, patterns, mine, other, consts):
    dft, kern, order = consts
    half = (2, W, W)
    return pl.pallas_call(
        backward_kernel,
        grid_spec=pltpu.PrefetchScalarGridSpec(
            num_scalar_prefetch=1,
            grid=(2,),
            in_specs=[
                stepped(PAIR, 0),
                stepped(PAIR, 0),
                stepped(PAIR, 0),
                fixed((W, W)),
                fixed((W, W)),
                pl.BlockSpec((1, W, W), lambda g, info: (info[3], 0, 0)),
                fixed(half),
                fixed(half),
                fixed(half),
                fixed(half),
                fixed((128, 128)),
            ],
            out_specs=[fixed(PAIR), stepped(BLOCKS, 1)],
            scratch_shapes=[VMEM(PAIR, BF16), VMEM((2 * W, 2 * W), BF16), VMEM((2 * W, 2 * W), BF16)],
        ),
        out_shape=[shape(PAIR, F32), shape(ALL_BLOCKS, BF16)],
        compiler_params=pltpu.CompilerParams(dimension_semantics=("arbitrary",), vmem_limit_bytes=28 << 20),
    )(info, psi, inc, far, power_a, power_b, patterns, mine, other, dft, kern, order)


def swap(value, axis):
    return lax.ppermute(value, axis, [(0, 1), (1, 0)])


def from_tile(value, distance):
    route = [(t + distance, t) for t in range(TILES) if 0 <= t + distance < TILES]
    return lax.ppermute(value, TILE_AXES, route)


def exchange(value, axes):
    return lax.all_to_all(value, axes, 0, 0, tiled=True)


def spread(value, axes, count):
    return exchange(jnp.broadcast_to(value[None], (count,) + value.shape), axes)


def update(
    object_tiles,
    object_previous,
    probe,
    probe_previous,
    patterns,
    offsets,
    scan_of_slot,
    tile_load,
    step_sizes,
    object_norm_before,
    probe_norm_before,
):
    core = lax.axis_index("c")
    slot = lax.axis_index("yh")
    dft, kern, order = tables()
    consts = (
        jnp.asarray(dft, BF16),
        jnp.asarray(kern, F32),
        jnp.asarray(order, BF16),
    )
    my_offset = lax.dynamic_index_in_dim(offsets, slot, 1, keepdims=False)
    used = (slot < tile_load[0]).astype(jnp.int32)
    info = jnp.stack([my_offset[0], my_offset[1], core.astype(jnp.int32), slot.astype(jnp.int32), used])
    columns = lax.broadcasted_iota(jnp.int32, (1, 1, W), 2)
    my_left = columns >= my_offset[1]

    zeros = jnp.zeros((1, 128), jnp.int32)
    here = 2 * (NX * lax.axis_index("yl") + lax.axis_index("x"))
    row = lax.dynamic_update_slice(zeros, offsets.reshape(1, 4), (0, 64))
    row = lax.dynamic_update_slice(row, scan_of_slot[None], (0, here))
    base_row = row
    rows = [row]
    for d in range(1, NX):
        rows.append(lax.ppermute(row, "x", [((x + d) % NX, x) for x in range(NX)]))
    row = sum(rows[1:], rows[0])
    row = row + swap(row, "yl")
    ids = row[0, : NYLX * NYH]

    own = lax.dynamic_index_in_dim(object_tiles[0], core, 0, keepdims=False).astype(BF16)
    above_row = from_tile(base_row, -TGX)
    above_col = lax.dynamic_slice(above_row, (0, 66 + slot), (1, 1)).reshape(1, 1, 1)
    above_left = columns >= above_col
    east = from_tile(own, 1)
    south = from_tile(jnp.where(above_left, own, east), TGX)

    rows = probe.astype(BF16).reshape(SCANS * 16, W)
    banded = spread(rows, "z", NZ).reshape(NZ, SCANS, 16, W)
    picked = whole(pick_kernel, shape((NYLX * NYH, NZ, 16, W), BF16), ids, [banded])
    blocks = exchange(picked, PLANE).reshape(ALL_BLOCKS)

    mine = whole(patch_kernel, shape((2, W, W), BF16), info, [own, east, south])
    other = swap(mine, "c")

    psi, inc, far, power = forward(info, blocks, mine, other, consts)
    power_other = swap(power, "c")
    terms, probe_terms = backward(info, psi, inc, far, power, power_other, patterns, mine, other, consts)

    theirs = swap(terms[1].astype(BF16), "c")
    half = (2, W, W)
    up, low = whole(place_kernel, [shape(half, F32), shape(half, BF16)], info, [terms[0], theirs])
    from_above = from_tile(low, -TGX).astype(F32)
    kept = jnp.where(my_left, up, 0.0) + jnp.where(above_left, from_above, 0.0)
    right = jnp.where(my_left, 0.0, up) + jnp.where(above_left, 0.0, from_above)
    from_left = from_tile(right.astype(BF16), -1)
    received = exchange(probe_terms.reshape(NYLX * NYH, NZ, 16, W), PLANE)
    by_scan = plain(scan_sum_kernel, shape((NZ, SCANS * 16, W), BF16), received, row)
    layer_part = (kept + from_left.astype(F32)).astype(BF16)
    layer_grad = layer_part.astype(F32) + swap(layer_part, "yh").astype(F32)
    summed = exchange(by_scan, "z")
    probe_grad, packed = plain(grad_sum_kernel, [shape((SCANS * 16, W), F32), shape((1, 128), F32)], summed, layer_grad)
    probe_grad = probe_grad.reshape(SCANS, 2, 2, ROWS, W)
    packed = jnp.sum(spread(packed, ("z",) + PLANE + ("c",), 4 * TILES), axis=0)
    object_square = packed[0, 0] / float(NYH * TILES * LAYERS * 2 * W * W)
    probe_square = packed[0, 1] / float(SCANS * MODES * 2 * W * W)
    other_grad = swap(layer_grad, "c")
    first = core == 0
    tile_grad = jnp.stack(
        [jnp.where(first, layer_grad, other_grad), jnp.where(first, other_grad, layer_grad)]
    )

    object_direction = -tile_grad[None] + object_square / object_norm_before[0] * object_previous
    new_object = object_tiles + step_sizes[0].astype(F32) / 1024.0 * object_direction
    probe_direction = -probe_grad + probe_square / probe_norm_before[0] * probe_previous
    new_probe = probe + step_sizes[1].astype(F32) / 16384.0 * probe_direction
    return (new_object, object_direction, new_probe, probe_direction)


def solution(mesh):
    fine = Mesh(mesh.devices.reshape(NZ, NYL, NX, NYH, NC), ("z", "yl", "x", "yh", "c"))
    tile, mode = TILE_AXES, ("yh", "c")
    objects = P(tile, None, None, None, None)
    probes = P(None, mode, None, tile, None)
    return jax.shard_map(
        update,
        mesh=fine,
        in_specs=(
            objects,
            objects,
            probes,
            probes,
            P(tile, None, None),
            P(None, tile),
            P(tile),
            P(tile),
            P(),
            P(),
            P(),
        ),
        out_specs=(objects, objects, probes, probes),
        check_vma=False,
    )
```

```python
import math

import jax
import jax.numpy as jnp
import numpy as np
from jax import lax
from jax.experimental import pallas as pl
from jax.experimental.pallas import tpu as pltpu
from jax.sharding import Mesh, PartitionSpec as P

TGX = 8
LAYERS = 2
MODES = 8
SCANS = 4
W = 256
NZ, NYL, NX, NYH, NC = 8, 2, 4, 2, 2
NYLX = NYL * NX
TILES = NZ * NYLX
ROWS = W // TILES
BAND = NYLX * ROWS
TILE_AXES = ("z", "yl", "x")
PLANE = ("yl", "x", "yh")
VMEM = pltpu.VMEM
F32 = jnp.float32
BF16 = jnp.bfloat16


def tables():
    index = np.arange(W, dtype=np.int64)
    angle = ((index[:, None] * index[None, :]) % W).astype(np.float32) * np.float32(2.0 * math.pi / W)
    factor = np.float32(1.0 / math.sqrt(W))
    cosine = np.cos(angle, dtype=np.float32) * factor
    sine = -np.sin(angle, dtype=np.float32) * factor
    dft = np.stack([cosine, sine])
    free = np.where(index < W // 2, index, index - W).astype(np.float32)
    phase = (free[:, None] * free[:, None] + free[None, :] * free[None, :]) * np.float32(math.pi / (4.0 * W))
    kernel = np.stack([np.cos(phase, dtype=np.float32), np.sin(phase, dtype=np.float32)])
    return dft, kernel


def mm(a, b):
    return jnp.dot(a, b, preferred_element_type=F32)


def transform(pairs, right, left):
    across = jnp.concatenate([jnp.concatenate(p, axis=1) for p in pairs], axis=0)
    first = mm(across.astype(BF16), right).astype(BF16)
    spans = [slice(i * W, (i + 1) * W) for i in range(len(pairs))]
    down = jnp.concatenate(
        [
            jnp.concatenate([first[at, :W] for at in spans], axis=1),
            jnp.concatenate([first[at, W:] for at in spans], axis=1),
        ],
        axis=0,
    )
    out = mm(left, down).astype(BF16)
    return [(out[:W, at], out[W:, at]) for at in spans]


def times(a_re, a_im, b_re, b_im):
    a_re, a_im, b_re, b_im = (v.astype(F32) for v in (a_re, a_im, b_re, b_im))
    return a_re * b_re - a_im * b_im, a_re * b_im + a_im * b_re


def conj_times(a_re, a_im, b_re, b_im):
    a_re, a_im, b_re, b_im = (v.astype(F32) for v in (a_re, a_im, b_re, b_im))
    return a_re * b_re + a_im * b_im, a_re * b_im - a_im * b_re


def placing(axis):
    natural = lax.broadcasted_iota(jnp.int32, (128, 128), axis)
    rows = lax.broadcasted_iota(jnp.int32, (128, 128), 1 - axis)
    band, i, ri, r = rows // 16, rows // 8 % 2, rows // 4 % 2, rows % 4
    return (natural == i * 64 + ri * 32 + band * 4 + r).astype(F32).astype(BF16)


def fill(step, dft, plus, minus):
    @pl.when(step == 0)
    def _():
        for i in range(2):
            at = slice(i * W, (i + 1) * W)
            plus[at, at] = dft[0]
            minus[at, at] = dft[0]
        for ref, a, b in ((plus, dft[1], -dft[1]), (minus, -dft[1], dft[1])):
            ref[:W, W:] = a
            ref[W:, :W] = b


def window_masks(row, col):
    rows = lax.broadcasted_iota(jnp.int32, (W, W), 0)
    cols = lax.broadcasted_iota(jnp.int32, (W, W), 1)
    return rows >= row, cols >= col


def patch_kernel(info, mixed, out):
    row, col = info[0], info[1]
    for ri in range(2):
        value = mixed[ri].astype(F32)
        value = pltpu.roll(value, (W - row) % W, 0)
        value = pltpu.roll(value, (W - col) % W, 1)
        out[ri] = value.astype(BF16)


def pick_kernel(ids, src, out):
    for d in range(NYLX * NYH):
        out[d] = src[:, ids[d]]


def forward_kernel(info, blocks, mine, other, dft, kern, psi, inc, far, power, plus, minus):
    step = pl.program_id(0)
    first = info[2] == 0
    fill(step, dft, plus, minus)
    order = placing(0)
    for z in range(NZ):
        piece = blocks[:, 0, z].reshape(128, W)
        placed = mm(order, piece).astype(BF16)
        for i in range(2):
            for ri in range(2):
                at = i * 64 + ri * 32
                psi[i, ri, z * BAND : (z + 1) * BAND] = placed[at : at + BAND]
    fwd, inv = plus[...], minus[...]
    p0 = [jnp.where(first, mine[ri], other[ri]) for ri in range(2)]
    p1 = [jnp.where(first, other[ri], mine[ri]) for ri in range(2)]
    pairs = range(2)
    spec = transform([times(psi[i, 0], psi[i, 1], *p0) for i in pairs], fwd, inv)
    moved = transform([times(*spec[i], kern[0], kern[1]) for i in pairs], inv, fwd)
    for i in pairs:
        inc[i, 0], inc[i, 1] = moved[i]
    waves = transform([times(*moved[i], *p1) for i in pairs], fwd, inv)
    total = None
    for i in pairs:
        far[i, 0], far[i, 1] = waves[i]
        f_re, f_im = waves[i][0].astype(F32), waves[i][1].astype(F32)
        part = f_re * f_re + f_im * f_im
        total = part if total is None else total + part

    @pl.when(step == 0)
    def _():
        power[...] = total

    @pl.when(step != 0)
    def _():
        power[...] += total


def backward_kernel(
    info, psi, inc, far, power_a, power_b, pattern, mine, other, dft, kern, terms, out, scratch, plus, minus
):
    step = pl.program_id(0)
    core = info[2]
    first = core == 0
    fill(step, dft, plus, minus)
    used = info[4].astype(F32)
    fwd, inv = plus[...], minus[...]
    p0 = [jnp.where(first, mine[ri], other[ri]) for ri in range(2)]
    p1 = [jnp.where(first, other[ri], mine[ri]) for ri in range(2)]
    double = 2.0 * ((power_a[...] + power_b[...] - pattern[0]) * used)
    pairs = range(2)
    back = transform([[double * far[i, ri].astype(F32) for ri in range(2)] for i in pairs], inv, fwd)
    term1 = [conj_times(inc[i, 0], inc[i, 1], *back[i]) for i in pairs]
    spec = transform([conj_times(*p1, *back[i]) for i in pairs], fwd, inv)
    back = transform([times(*spec[i], kern[0], -kern[1]) for i in pairs], inv, fwd)
    term0 = [conj_times(psi[i, 0], psi[i, 1], *back[i]) for i in pairs]
    for i in pairs:
        for ri, value in enumerate(conj_times(*p0, *back[i])):
            scratch[i, ri] = value.astype(BF16)
    sums = [t[0][ri] + t[1][ri] for t in (term0, term1) for ri in range(2)]
    back = placing(1)
    for z in range(NZ):
        pieces = [
            scratch[i, ri, z * BAND : (z + 1) * BAND] for i in range(2) for ri in range(2)
        ]
        piece = mm(back, jnp.concatenate(pieces, axis=0)).astype(BF16)
        out[:, 0, z] = piece.reshape(NYLX, 16, W)
    for layer in range(LAYERS):
        slot = core if layer == 0 else 1 - core

        @pl.when(step == 0)
        def _():
            terms[slot, 0] = sums[2 * layer]
            terms[slot, 1] = sums[2 * layer + 1]

        @pl.when(step != 0)
        def _():
            terms[slot, 0] += sums[2 * layer]
            terms[slot, 1] += sums[2 * layer + 1]


def place_kernel(info, own, other, kept, right, low):
    zero = jnp.zeros((W, W), F32)
    parts = [zero] * 4
    for window, at in ((own, 0), (other, 5)):
        row, col = info[at], info[at + 1]
        upper, left = window_masks(row, col)
        value = pltpu.roll(window[...].astype(F32), row, 0)
        value = pltpu.roll(value, col, 1)
        top, down = jnp.where(upper, value, zero), jnp.where(upper, zero, value)
        pieces = [p for v in (top, down) for p in (jnp.where(left, v, zero), jnp.where(left, zero, v))]
        parts = [p + q for p, q in zip(parts, pieces)]
    kept[...], right[...] = parts[0], parts[1]
    low[0], low[1] = parts[2].astype(BF16), parts[3].astype(BF16)


def scan_sum_kernel(src, ids, out):
    wide = NYLX * NYH * 16
    spread_of = lax.broadcasted_iota(jnp.int32, (128, wide), 1) // 16
    expand = (spread_of == lax.broadcasted_iota(jnp.int32, (128, wide), 0)).astype(BF16)
    idrow = jnp.broadcast_to(ids[...], (8, 128)).astype(F32).astype(BF16)
    scan = mm(idrow, expand)[:1]
    target = lax.broadcasted_iota(jnp.int32, (SCANS * 16, wide), 0)
    column = lax.broadcasted_iota(jnp.int32, (SCANS * 16, wide), 1)
    take = (scan == (target // 16).astype(F32)) & (target % 16 == column % 16)
    take = take.astype(BF16)
    for z in range(NZ):
        out[z] = mm(take, src[:, z].reshape(wide, W)).astype(BF16)


def grad_sum_kernel(src, layer, out, packed):
    total = src[0].astype(F32)
    for z in range(1, NZ):
        total += src[z].astype(F32)
    out[...] = total
    object_part = jnp.sum(layer[...] * layer[...])
    probe_part = jnp.sum(total * total)
    lane = lax.broadcasted_iota(jnp.int32, (1, 128), 1)
    packed[...] = jnp.where(lane == 0, object_part, probe_part)


def finish_kernel(
    info, steps, object_norm, probe_norm, packed, layer, other, tiles, before, grad, probe, probe_before, *outs
):
    new_tiles, direction, new_probe, probe_direction, held, sems = outs
    totals = jnp.sum(packed[...].reshape(4 * TILES, 128), axis=0, keepdims=True)
    lane = lax.broadcasted_iota(jnp.int32, (1, 128), 1)

    def square(at, count):
        return jnp.sum(jnp.where(lane == at, totals, 0.0), axis=1, keepdims=True) / float(count)

    ratio = square(0, TILES * LAYERS * 2 * W * W) / object_norm[0]
    rate = steps[0].astype(F32) / 1024.0
    copies = []
    for l in range(LAYERS):
        for ri in range(2):
            gradient = jnp.where(info[2] == l, layer[ri], other[ri])
            turned = ratio * before[0, l, ri] - gradient
            held[1, l, ri] = turned
            held[0, l, ri] = tiles[0, l, ri] + rate * turned
            for k, target in enumerate((new_tiles, direction)):
                copies.append(pltpu.make_async_copy(held.at[k, l, ri], target.at[0, l, ri], sems.at[k, l, ri]))
                copies[-1].start()
    ratio = square(1, SCANS * MODES * 2 * W * W) / probe_norm[0]
    probe_rate = steps[1].astype(F32) / 16384.0
    for s in range(SCANS):
        for i in range(2):
            for ri in range(2):
                at = ROWS * (4 * s + 2 * i + ri)
                value = ratio * probe_before[s, i, ri] - grad[at : at + ROWS]
                probe_direction[s, i, ri] = value
                new_probe[s, i, ri] = probe[s, i, ri] + probe_rate * value
    for copy in copies:
        copy.wait()


def finish(scalars, arrays):
    spec = pl.BlockSpec(memory_space=VMEM)
    away = pl.BlockSpec(memory_space=pl.ANY)
    return pl.pallas_call(
        finish_kernel,
        grid_spec=pltpu.PrefetchScalarGridSpec(
            num_scalar_prefetch=4,
            grid=(),
            in_specs=[spec] * len(arrays),
            out_specs=[away, away, spec, spec],
            scratch_shapes=[VMEM((2, LAYERS, 2, W, W), F32), pltpu.SemaphoreType.DMA((2, LAYERS, 2))],
        ),
        out_shape=[shape((1, LAYERS, 2, W, W), F32)] * 2 + [shape((SCANS, 2, 2, ROWS, W), F32)] * 2,
        compiler_params=pltpu.CompilerParams(vmem_limit_bytes=16 << 20),
    )(*scalars, *arrays)


def plain(kernel, out_shape, *arrays):
    spec = pl.BlockSpec(memory_space=VMEM)
    single = not isinstance(out_shape, (list, tuple))
    return pl.pallas_call(
        kernel,
        in_specs=[spec] * len(arrays),
        out_specs=spec if single else [spec] * len(out_shape),
        out_shape=out_shape,
        compiler_params=pltpu.CompilerParams(vmem_limit_bytes=8 << 20),
    )(*arrays)


def shape(dims, dtype):
    return jax.ShapeDtypeStruct(dims, dtype)


def whole(kernel, out_shape, scalars, arrays, scratch=()):
    spec = pl.BlockSpec(memory_space=VMEM)
    single = not isinstance(out_shape, (list, tuple))
    return pl.pallas_call(
        kernel,
        grid_spec=pltpu.PrefetchScalarGridSpec(
            num_scalar_prefetch=1,
            grid=(),
            in_specs=[spec] * len(arrays),
            out_specs=spec if single else [spec] * len(out_shape),
            scratch_shapes=list(scratch),
        ),
        out_shape=out_shape,
        compiler_params=pltpu.CompilerParams(vmem_limit_bytes=8 << 20),
    )(scalars, *arrays)


def fixed(dims):
    return pl.BlockSpec(dims, lambda g, info: (0,) * len(dims))


def stepped(dims, axis):
    return pl.BlockSpec(dims, lambda g, info: tuple(g if a == axis else 0 for a in range(len(dims))))


PAIR = (2, 2, W, W)
BLOCKS = (NYLX, 1, NZ, 16, W)
ALL_BLOCKS = (NYLX, NYH, NZ, 16, W)


def forward(info, blocks, mine, other, consts):
    dft, kern = consts
    half = (2, W, W)
    return pl.pallas_call(
        forward_kernel,
        grid_spec=pltpu.PrefetchScalarGridSpec(
            num_scalar_prefetch=1,
            grid=(2,),
            in_specs=[
                stepped(BLOCKS, 1),
                fixed(half),
                fixed(half),
                fixed(half),
                fixed(half),
            ],
            out_specs=[stepped(PAIR, 0), stepped(PAIR, 0), stepped(PAIR, 0), fixed((W, W))],
            scratch_shapes=[VMEM((2 * W, 2 * W), BF16), VMEM((2 * W, 2 * W), BF16)],
        ),
        out_shape=[shape((4, 2, W, W), BF16)] * 3 + [shape((W, W), F32)],
        compiler_params=pltpu.CompilerParams(dimension_semantics=("arbitrary",), vmem_limit_bytes=28 << 20),
    )(info, blocks, mine, other, dft, kern)


def backward(info, psi, inc, far, power_a, power_b, patterns, mine, other, consts):
    dft, kern = consts
    half = (2, W, W)
    return pl.pallas_call(
        backward_kernel,
        grid_spec=pltpu.PrefetchScalarGridSpec(
            num_scalar_prefetch=1,
            grid=(2,),
            in_specs=[
                stepped(PAIR, 0),
                stepped(PAIR, 0),
                stepped(PAIR, 0),
                fixed((W, W)),
                fixed((W, W)),
                pl.BlockSpec((1, W, W), lambda g, info: (info[3], 0, 0)),
                fixed(half),
                fixed(half),
                fixed(half),
                fixed(half),
            ],
            out_specs=[fixed(PAIR), stepped(BLOCKS, 1)],
            scratch_shapes=[VMEM(PAIR, BF16), VMEM((2 * W, 2 * W), BF16), VMEM((2 * W, 2 * W), BF16)],
        ),
        out_shape=[shape(PAIR, F32), shape(ALL_BLOCKS, BF16)],
        compiler_params=pltpu.CompilerParams(dimension_semantics=("arbitrary",), vmem_limit_bytes=28 << 20),
    )(info, psi, inc, far, power_a, power_b, patterns, mine, other, dft, kern)


def swap(value, axis):
    return lax.ppermute(value, axis, [(0, 1), (1, 0)])


def from_tile(value, distance):
    route = [(t + distance, t) for t in range(TILES) if 0 <= t + distance < TILES]
    return lax.ppermute(value, TILE_AXES, route)


def exchange(value, axes):
    return lax.all_to_all(value, axes, 0, 0, tiled=True)


def spread(value, axes, count):
    return exchange(jnp.broadcast_to(value[None], (count,) + value.shape), axes)


def update(
    object_tiles,
    object_previous,
    probe,
    probe_previous,
    patterns,
    offsets,
    scan_of_slot,
    tile_load,
    step_sizes,
    object_norm_before,
    probe_norm_before,
):
    core = lax.axis_index("c")
    slot = lax.axis_index("yh")
    dft, kern = tables()
    consts = (
        jnp.asarray(dft, BF16),
        jnp.asarray(kern, F32),
    )
    my_offset = lax.dynamic_index_in_dim(offsets, slot, 1, keepdims=False)
    used = (slot < tile_load[0]).astype(jnp.int32)
    twin_offset = lax.dynamic_index_in_dim(offsets, 1 - slot, 1, keepdims=False)
    info = jnp.concatenate(
        [my_offset, jnp.stack([core.astype(jnp.int32), slot.astype(jnp.int32), used]), twin_offset]
    )
    columns = lax.broadcasted_iota(jnp.int32, (1, 1, W), 2)
    lines = lax.broadcasted_iota(jnp.int32, (1, W, 1), 1)
    my_upper, my_left = lines >= my_offset[0], columns >= my_offset[1]

    zeros = jnp.zeros((1, 128), jnp.int32)
    here = 2 * (NX * lax.axis_index("yl") + lax.axis_index("x"))
    row = lax.dynamic_update_slice(zeros, scan_of_slot[None], (0, here))
    rows = [row]
    for d in range(1, NX):
        rows.append(lax.ppermute(row, "x", [((x + d) % NX, x) for x in range(NX)]))
    row = sum(rows[1:], rows[0])
    row = row + swap(row, "yl")
    ids = row[0, : NYLX * NYH]

    own = lax.dynamic_index_in_dim(object_tiles[0], core, 0, keepdims=False).astype(BF16)
    above_row = from_tile(jnp.pad(offsets.reshape(1, 4), ((0, 0), (0, 124))), -TGX)
    above_col = lax.dynamic_slice(above_row, (0, 2 + slot), (1, 1)).reshape(1, 1, 1)
    above_left = columns >= above_col
    east = from_tile(own, 1)
    south = from_tile(jnp.where(above_left, own, east), TGX)

    rows = probe.astype(BF16).reshape(SCANS * 16, W)
    banded = spread(rows, "z", NZ).reshape(NZ, SCANS, 16, W)
    picked = whole(pick_kernel, shape((NYLX * NYH, NZ, 16, W), BF16), ids, [banded])
    blocks = exchange(picked, PLANE).reshape(ALL_BLOCKS)

    mixed = jnp.where(my_upper, jnp.where(my_left, own, east), south)
    mine = whole(patch_kernel, shape((2, W, W), BF16), info, [mixed])
    other = swap(mine, "c")

    psi, inc, far, power = forward(info, blocks, mine, other, consts)
    power_other = swap(power, "c")
    terms, probe_terms = backward(info, psi, inc, far, power, power_other, patterns, mine, other, consts)

    summed = terms[0] + swap(terms[1].astype(BF16), "c").astype(F32)
    real = slot == 0
    window = jnp.where(real, summed[0], summed[1])
    twin = swap(jnp.where(real, summed[1], summed[0]).astype(BF16), "yh")
    field = shape((W, W), F32)
    kept, right, low = whole(
        place_kernel, [field, field, shape((2, W, W), BF16)], info, [window, twin]
    )
    from_above = from_tile(low, -TGX).astype(F32)
    kept = kept + from_above[0]
    right = right + from_above[1]
    received = exchange(probe_terms.reshape(NYLX * NYH, NZ, 16, W), PLANE)
    by_scan = plain(scan_sum_kernel, shape((NZ, SCANS * 16, W), BF16), received, row)
    part_grad = kept + from_tile(right.astype(BF16), -1).astype(F32)
    summed = exchange(by_scan, "z")
    probe_grad, packed = plain(grad_sum_kernel, [shape((SCANS * 16, W), F32), shape((1, 128), F32)], summed, part_grad)
    packed = spread(packed, ("z",) + PLANE + ("c",), 4 * TILES)
    twin_part = swap(part_grad, "yh")
    layer_grad = jnp.stack(
        [jnp.where(real, part_grad, twin_part), jnp.where(real, twin_part, part_grad)]
    )
    other_grad = swap(layer_grad, "c")

    return finish(
        (info, step_sizes, object_norm_before, probe_norm_before),
        (packed, layer_grad, other_grad, object_tiles, object_previous, probe_grad, probe, probe_previous),
    )


def solution(mesh):
    fine = Mesh(mesh.devices.reshape(NZ, NYL, NX, NYH, NC), ("z", "yl", "x", "yh", "c"))
    tile, mode = TILE_AXES, ("yh", "c")
    objects = P(tile, None, None, None, None)
    probes = P(None, mode, None, tile, None)
    return jax.shard_map(
        update,
        mesh=fine,
        in_specs=(
            objects,
            objects,
            probes,
            probes,
            P(tile, None, None),
            P(None, tile),
            P(tile),
            P(tile),
            P(),
            P(),
            P(),
        ),
        out_specs=(objects, objects, probes, probes),
        check_vma=False,
    )
```

```python
import math

import jax
import jax.numpy as jnp
import numpy as np
from jax import lax
from jax.experimental import pallas as pl
from jax.experimental.pallas import tpu as pltpu
from jax.sharding import Mesh, PartitionSpec as P

TGX = 8
LAYERS = 2
MODES = 8
SCANS = 4
W = 256
NZ, NYL, NX, NYH, NC = 8, 2, 4, 2, 2
NYLX = NYL * NX
TILES = NZ * NYLX
ROWS = W // TILES
BAND = NYLX * ROWS
TILE_AXES = ("z", "yl", "x")
PLANE = ("yl", "x", "yh")
VMEM = pltpu.VMEM
F32 = jnp.float32
BF16 = jnp.bfloat16


def tables():
    index = np.arange(W, dtype=np.int64)
    angle = ((index[:, None] * index[None, :]) % W).astype(np.float32) * np.float32(2.0 * math.pi / W)
    factor = np.float32(1.0 / math.sqrt(W))
    cosine = np.cos(angle, dtype=np.float32) * factor
    sine = -np.sin(angle, dtype=np.float32) * factor
    dft = np.stack([cosine, sine])
    free = np.where(index < W // 2, index, index - W).astype(np.float32)
    phase = (free[:, None] * free[:, None] + free[None, :] * free[None, :]) * np.float32(math.pi / (4.0 * W))
    kernel = np.stack([np.cos(phase, dtype=np.float32), np.sin(phase, dtype=np.float32)])
    return dft, kernel


def mm(a, b):
    return jnp.dot(a, b, preferred_element_type=F32)


def transform(pairs, right, left):
    across = jnp.concatenate([jnp.concatenate(p, axis=1) for p in pairs], axis=0)
    first = mm(across.astype(BF16), right).astype(BF16)
    spans = [slice(i * W, (i + 1) * W) for i in range(len(pairs))]
    down = jnp.concatenate(
        [
            jnp.concatenate([first[at, :W] for at in spans], axis=1),
            jnp.concatenate([first[at, W:] for at in spans], axis=1),
        ],
        axis=0,
    )
    out = mm(left, down).astype(BF16)
    return [(out[:W, at], out[W:, at]) for at in spans]


def times(a_re, a_im, b_re, b_im):
    a_re, a_im, b_re, b_im = (v.astype(F32) for v in (a_re, a_im, b_re, b_im))
    return a_re * b_re - a_im * b_im, a_re * b_im + a_im * b_re


def conj_times(a_re, a_im, b_re, b_im):
    a_re, a_im, b_re, b_im = (v.astype(F32) for v in (a_re, a_im, b_re, b_im))
    return a_re * b_re + a_im * b_im, a_re * b_im - a_im * b_re


def placing(axis):
    natural = lax.broadcasted_iota(jnp.int32, (128, 128), axis)
    rows = lax.broadcasted_iota(jnp.int32, (128, 128), 1 - axis)
    band, i, ri, r = rows // 16, rows // 8 % 2, rows // 4 % 2, rows % 4
    return (natural == i * 64 + ri * 32 + band * 4 + r).astype(F32).astype(BF16)


def fill(dft, plus, minus):
    for i in range(2):
        at = slice(i * W, (i + 1) * W)
        plus[at, at] = dft[0]
        minus[at, at] = dft[0]
    for ref, a, b in ((plus, dft[1], -dft[1]), (minus, -dft[1], dft[1])):
        ref[:W, W:] = a
        ref[W:, :W] = b


def window_masks(row, col):
    rows = lax.broadcasted_iota(jnp.int32, (W, W), 0)
    cols = lax.broadcasted_iota(jnp.int32, (W, W), 1)
    return rows >= row, cols >= col


def choose_kernel(above, own, east, out):
    col = above[2 + lax.axis_index("yh")]
    left = lax.broadcasted_iota(jnp.int32, (W, W), 1) >= col
    for ri in range(2):
        out[ri] = jnp.where(left, own[ri].astype(F32), east[ri].astype(F32)).astype(BF16)


def patch_kernel(info, mixed, out):
    row, col = info[0], info[1]
    for ri in range(2):
        value = mixed[ri].astype(F32)
        value = pltpu.roll(value, (W - row) % W, 0)
        value = pltpu.roll(value, (W - col) % W, 1)
        out[ri] = value.astype(BF16)


def pick_kernel(ids, src, out):
    for d in range(NYLX * NYH):
        out[d] = src[:, ids[d]]


def forward_kernel(info, blocks, mine, other, dft, kern, all_psi, all_inc, all_far, power, plus, minus):
    first = info[2] == 0
    fill(dft, plus, minus)
    order = placing(0)
    power[...] = jnp.zeros_like(power)

    def pair(g, carry):
        psi, inc, far = (ref.at[pl.ds(2 * g, 2)] for ref in (all_psi, all_inc, all_far))
        for z in range(NZ):
            piece = blocks[:, g, z].reshape(128, W)
            placed = mm(order, piece).astype(BF16)
            for i in range(2):
                for ri in range(2):
                    at = i * 64 + ri * 32
                    psi[i, ri, z * BAND : (z + 1) * BAND] = placed[at : at + BAND]
        fwd, inv = plus[...], minus[...]
        p0 = [jnp.where(first, mine[ri], other[ri]) for ri in range(2)]
        p1 = [jnp.where(first, other[ri], mine[ri]) for ri in range(2)]
        pairs = range(2)
        spec = transform([times(psi[i, 0], psi[i, 1], *p0) for i in pairs], fwd, inv)
        moved = transform([times(*spec[i], kern[0], kern[1]) for i in pairs], inv, fwd)
        for i in pairs:
            inc[i, 0], inc[i, 1] = moved[i]
        waves = transform([times(*moved[i], *p1) for i in pairs], fwd, inv)
        total = power[...]
        for i in pairs:
            far[i, 0], far[i, 1] = waves[i]
            f_re, f_im = waves[i][0].astype(F32), waves[i][1].astype(F32)
            total = total + (f_re * f_re + f_im * f_im)
        power[...] = total
        return carry

    lax.fori_loop(0, 2, pair, 0)


def backward_kernel(info, *refs):
    all_psi, all_inc, all_far, power_a, power_b, patterns, mine, other, dft, kern = refs[:10]
    terms, out, scratch, plus, minus = refs[10:]
    core = info[2]
    first = core == 0
    fill(dft, plus, minus)
    used = info[4].astype(F32)
    back_order = placing(1)
    terms[...] = jnp.zeros_like(terms)

    def pair(g, carry):
        psi, inc, far = (ref.at[pl.ds(2 * g, 2)] for ref in (all_psi, all_inc, all_far))
        fwd, inv = plus[...], minus[...]
        p0 = [jnp.where(first, mine[ri], other[ri]) for ri in range(2)]
        p1 = [jnp.where(first, other[ri], mine[ri]) for ri in range(2)]
        double = 2.0 * ((power_a[...] + power_b[...] - patterns[info[3]]) * used)
        pairs = range(2)
        back = transform([[double * far[i, ri].astype(F32) for ri in range(2)] for i in pairs], inv, fwd)
        term1 = [conj_times(inc[i, 0], inc[i, 1], *back[i]) for i in pairs]
        spec = transform([conj_times(*p1, *back[i]) for i in pairs], fwd, inv)
        back = transform([times(*spec[i], kern[0], -kern[1]) for i in pairs], inv, fwd)
        term0 = [conj_times(psi[i, 0], psi[i, 1], *back[i]) for i in pairs]
        for i in pairs:
            for ri, value in enumerate(conj_times(*p0, *back[i])):
                scratch[i, ri] = value.astype(BF16)
        for layer, term in enumerate((term0, term1)):
            slot = core if layer == 0 else 1 - core
            for ri in range(2):
                terms[slot, ri] += term[0][ri] + term[1][ri]
        for z in range(NZ):
            at = slice(z * BAND, (z + 1) * BAND)
            pieces = [scratch[i, ri, at] for i in range(2) for ri in range(2)]
            piece = mm(back_order, jnp.concatenate(pieces, axis=0)).astype(BF16)
            out[:, g, z] = piece.reshape(NYLX, 16, W)
        return carry

    lax.fori_loop(0, 2, pair, 0)


def place_kernel(info, own, other, kept, right, low):
    zero = jnp.zeros((W, W), F32)
    parts = [zero] * 4
    for window, at in ((own, 0), (other, 5)):
        row, col = info[at], info[at + 1]
        upper, left = window_masks(row, col)
        value = pltpu.roll(window[...].astype(F32), row, 0)
        value = pltpu.roll(value, col, 1)
        top, down = jnp.where(upper, value, zero), jnp.where(upper, zero, value)
        pieces = [p for v in (top, down) for p in (jnp.where(left, v, zero), jnp.where(left, zero, v))]
        parts = [p + q for p, q in zip(parts, pieces)]
    kept[...], right[...] = parts[0], parts[1]
    low[0], low[1] = parts[2].astype(BF16), parts[3].astype(BF16)


def scan_sum_kernel(src, ids, out):
    wide = NYLX * NYH * 16
    spread_of = lax.broadcasted_iota(jnp.int32, (128, wide), 1) // 16
    expand = (spread_of == lax.broadcasted_iota(jnp.int32, (128, wide), 0)).astype(BF16)
    idrow = jnp.broadcast_to(ids[...], (8, 128)).astype(F32).astype(BF16)
    scan = mm(idrow, expand)[:1]
    target = lax.broadcasted_iota(jnp.int32, (SCANS * 16, wide), 0)
    column = lax.broadcasted_iota(jnp.int32, (SCANS * 16, wide), 1)
    take = (scan == (target // 16).astype(F32)) & (target % 16 == column % 16)
    take = take.astype(BF16)
    for z in range(NZ):
        out[z] = mm(take, src[:, z].reshape(wide, W)).astype(BF16)


def grad_sum_kernel(src, layer, out, packed):
    total = src[0].astype(F32)
    for z in range(1, NZ):
        total += src[z].astype(F32)
    out[...] = total
    object_part = jnp.sum(layer[...] * layer[...])
    probe_part = jnp.sum(total * total)
    lane = lax.broadcasted_iota(jnp.int32, (1, 128), 1)
    packed[...] = jnp.where(lane == 0, object_part, probe_part)


def finish_kernel(
    info, steps, object_norm, probe_norm, packed, layer, other, tiles, before, grad, probe, probe_before, *outs
):
    new_tiles, direction, new_probe, probe_direction, held, fetched, sems, fetch_sem = outs
    fetch = pltpu.make_async_copy(other, fetched, fetch_sem)
    fetch.start()
    totals = jnp.sum(packed[...].reshape(4 * TILES, 128), axis=0, keepdims=True)
    lane = lax.broadcasted_iota(jnp.int32, (1, 128), 1)

    def square(at, count):
        return jnp.sum(jnp.where(lane == at, totals, 0.0), axis=1, keepdims=True) / float(count)

    ratio = square(0, TILES * LAYERS * 2 * W * W) / object_norm[0]
    rate = steps[0].astype(F32) / 1024.0
    copies = []
    for turn in range(LAYERS):
        l = info[2] if turn == 0 else 1 - info[2]
        if turn == 1:
            fetch.wait()
        for ri in range(2):
            turned = ratio * before[0, l, ri] - (layer, fetched)[turn][ri]
            held[1, turn, ri] = turned
            held[0, turn, ri] = tiles[0, l, ri] + rate * turned
            for k, target in enumerate((new_tiles, direction)):
                copies.append(pltpu.make_async_copy(held.at[k, turn, ri], target.at[0, l, ri], sems.at[k, turn, ri]))
                copies[-1].start()
    ratio = square(1, SCANS * MODES * 2 * W * W) / probe_norm[0]
    probe_rate = steps[1].astype(F32) / 16384.0
    for s in range(SCANS):
        for i in range(2):
            for ri in range(2):
                at = ROWS * (4 * s + 2 * i + ri)
                value = ratio * probe_before[s, i, ri] - grad[at : at + ROWS]
                probe_direction[s, i, ri] = value
                new_probe[s, i, ri] = probe[s, i, ri] + probe_rate * value
    for copy in copies:
        copy.wait()


def finish(scalars, arrays):
    spec = pl.BlockSpec(memory_space=VMEM)
    away = pl.BlockSpec(memory_space=pl.ANY)
    return pl.pallas_call(
        finish_kernel,
        grid_spec=pltpu.PrefetchScalarGridSpec(
            num_scalar_prefetch=4,
            grid=(),
            in_specs=[spec, spec, away] + [spec] * (len(arrays) - 3),
            out_specs=[away, away, spec, spec],
            scratch_shapes=[
                VMEM((2, LAYERS, 2, W, W), F32),
                VMEM((2, W, W), F32),
                pltpu.SemaphoreType.DMA((2, LAYERS, 2)),
                pltpu.SemaphoreType.DMA,
            ],
        ),
        out_shape=[shape((1, LAYERS, 2, W, W), F32)] * 2 + [shape((SCANS, 2, 2, ROWS, W), F32)] * 2,
        compiler_params=pltpu.CompilerParams(vmem_limit_bytes=16 << 20),
    )(*scalars, *arrays)


def plain(kernel, out_shape, *arrays):
    spec = pl.BlockSpec(memory_space=VMEM)
    single = not isinstance(out_shape, (list, tuple))
    return pl.pallas_call(
        kernel,
        in_specs=[spec] * len(arrays),
        out_specs=spec if single else [spec] * len(out_shape),
        out_shape=out_shape,
        compiler_params=pltpu.CompilerParams(vmem_limit_bytes=8 << 20),
    )(*arrays)


def shape(dims, dtype):
    return jax.ShapeDtypeStruct(dims, dtype)


def whole(kernel, out_shape, scalars, arrays, scratch=(), limit=8):
    spec = pl.BlockSpec(memory_space=VMEM)
    single = not isinstance(out_shape, (list, tuple))
    return pl.pallas_call(
        kernel,
        grid_spec=pltpu.PrefetchScalarGridSpec(
            num_scalar_prefetch=1,
            grid=(),
            in_specs=[spec] * len(arrays),
            out_specs=spec if single else [spec] * len(out_shape),
            scratch_shapes=list(scratch),
        ),
        out_shape=out_shape,
        compiler_params=pltpu.CompilerParams(vmem_limit_bytes=limit << 20),
    )(scalars, *arrays)


PAIR = (2, 2, W, W)
ALL_BLOCKS = (NYLX, NYH, NZ, 16, W)


MATRIX = VMEM((2 * W, 2 * W), BF16)


def forward(info, blocks, mine, other, consts):
    outs = [shape((4, 2, W, W), BF16)] * 3 + [shape((W, W), F32)]
    return whole(forward_kernel, outs, info, [blocks, mine, other, *consts], [MATRIX] * 2, 24)


def backward(info, psi, inc, far, power_a, power_b, patterns, mine, other, consts):
    outs = [shape(PAIR, F32), shape(ALL_BLOCKS, BF16)]
    arrays = [psi, inc, far, power_a, power_b, patterns, mine, other, *consts]
    return whole(backward_kernel, outs, info, arrays, [VMEM(PAIR, BF16), MATRIX, MATRIX], 24)


def swap(value, axis):
    return lax.ppermute(value, axis, [(0, 1), (1, 0)])


def from_tile(value, distance):
    route = [(t + distance, t) for t in range(TILES) if 0 <= t + distance < TILES]
    return lax.ppermute(value, TILE_AXES, route)


def exchange(value, axes):
    return lax.all_to_all(value, axes, 0, 0, tiled=True)


def spread(value, axes, count):
    return exchange(jnp.broadcast_to(value[None], (count,) + value.shape), axes)


def update(
    object_tiles,
    object_previous,
    probe,
    probe_previous,
    patterns,
    offsets,
    scan_of_slot,
    tile_load,
    step_sizes,
    object_norm_before,
    probe_norm_before,
):
    core = lax.axis_index("c")
    slot = lax.axis_index("yh")
    dft, kern = tables()
    consts = (
        jnp.asarray(dft, BF16),
        jnp.asarray(kern, F32),
    )
    my_offset = lax.dynamic_index_in_dim(offsets, slot, 1, keepdims=False)
    used = (slot < tile_load[0]).astype(jnp.int32)
    twin_offset = lax.dynamic_index_in_dim(offsets, 1 - slot, 1, keepdims=False)
    info = jnp.concatenate(
        [my_offset, jnp.stack([core.astype(jnp.int32), slot.astype(jnp.int32), used]), twin_offset]
    )
    columns = lax.broadcasted_iota(jnp.int32, (1, 1, W), 2)
    lines = lax.broadcasted_iota(jnp.int32, (1, W, 1), 1)
    my_upper, my_left = lines >= my_offset[0], columns >= my_offset[1]

    zeros = jnp.zeros((1, 128), jnp.int32)
    here = 2 * (NX * lax.axis_index("yl") + lax.axis_index("x"))
    row = lax.dynamic_update_slice(zeros, scan_of_slot[None], (0, here))
    rows = [row]
    for d in range(1, NX):
        rows.append(lax.ppermute(row, "x", [((x + d) % NX, x) for x in range(NX)]))
    row = sum(rows[1:], rows[0])
    row = row + swap(row, "yl")
    ids = row[0, : NYLX * NYH]

    own = lax.dynamic_index_in_dim(object_tiles[0], core, 0, keepdims=False).astype(BF16)
    above = from_tile(offsets, -TGX)
    east = from_tile(own, 1)
    chosen = whole(
        choose_kernel, shape((2, W, W), BF16), above.reshape(4), [own, east]
    )
    south = from_tile(chosen, TGX)

    rows = probe.astype(BF16).reshape(SCANS * 16, W)
    banded = spread(rows, "z", NZ).reshape(NZ, SCANS, 16, W)
    picked = whole(pick_kernel, shape((NYLX * NYH, NZ, 16, W), BF16), ids, [banded])
    blocks = exchange(picked, PLANE).reshape(ALL_BLOCKS)

    mixed = jnp.where(my_upper, jnp.where(my_left, own, east), south)
    mine = whole(patch_kernel, shape((2, W, W), BF16), info, [mixed])
    other = swap(mine, "c")

    psi, inc, far, power = forward(info, blocks, mine, other, consts)
    power_other = swap(power, "c")
    terms, probe_terms = backward(info, psi, inc, far, power, power_other, patterns, mine, other, consts)

    summed = terms[0] + swap(terms[1].astype(BF16), "c").astype(F32)
    real = slot == 0
    window = jnp.where(real, summed[0], summed[1])
    twin = swap(jnp.where(real, summed[1], summed[0]).astype(BF16), "yh")
    field = shape((W, W), F32)
    kept, right, low = whole(
        place_kernel, [field, field, shape((2, W, W), BF16)], info, [window, twin]
    )
    from_above = from_tile(low, -TGX).astype(F32)
    kept = kept + from_above[0]
    right = right + from_above[1]
    received = exchange(probe_terms.reshape(NYLX * NYH, NZ, 16, W), PLANE)
    by_scan = plain(scan_sum_kernel, shape((NZ, SCANS * 16, W), BF16), received, row)
    part_grad = kept + from_tile(right.astype(BF16), -1).astype(F32)
    summed = exchange(by_scan, "z")
    probe_grad, packed = plain(
        grad_sum_kernel, [shape((SCANS * 16, W), F32), shape((1, 128), F32)], summed, part_grad
    )
    packed = spread(packed, ("z",) + PLANE + ("c",), 4 * TILES)
    twin_part = swap(part_grad, "yh")
    layer_grad = jnp.stack(
        [jnp.where(real, part_grad, twin_part), jnp.where(real, twin_part, part_grad)]
    )
    other_grad = swap(layer_grad, "c")

    return finish(
        (info, step_sizes, object_norm_before, probe_norm_before),
        (packed, layer_grad, other_grad, object_tiles, object_previous, probe_grad, probe, probe_previous),
    )


def solution(mesh):
    fine = Mesh(mesh.devices.reshape(NZ, NYL, NX, NYH, NC), ("z", "yl", "x", "yh", "c"))
    tile, mode = TILE_AXES, ("yh", "c")
    objects = P(tile, None, None, None, None)
    probes = P(None, mode, None, tile, None)
    return jax.shard_map(
        update,
        mesh=fine,
        in_specs=(
            objects,
            objects,
            probes,
            probes,
            P(tile, None, None),
            P(None, tile),
            P(tile),
            P(tile),
            P(),
            P(),
            P(),
        ),
        out_specs=(objects, objects, probes, probes),
        check_vma=False,
    )
```

```python
import math

import jax
import jax.numpy as jnp
import numpy as np
from jax import lax
from jax.experimental import pallas as pl
from jax.experimental.pallas import tpu as pltpu
from jax.sharding import Mesh, PartitionSpec as P

TGX = 8
LAYERS = 2
MODES = 8
SCANS = 4
W = 256
NZ, NYL, NX, NYH, NC = 8, 2, 4, 2, 2
NYLX = NYL * NX
TILES = NZ * NYLX
ROWS = W // TILES
BAND = NYLX * ROWS
TILE_AXES = ("z", "yl", "x")
PLANE = ("yl", "x", "yh")
VMEM = pltpu.VMEM
F32 = jnp.float32
BF16 = jnp.bfloat16


def tables():
    index = np.arange(W, dtype=np.int64)
    angle = ((index[:, None] * index[None, :]) % W).astype(np.float32) * np.float32(2.0 * math.pi / W)
    factor = np.float32(1.0 / math.sqrt(W))
    cosine = np.cos(angle, dtype=np.float32) * factor
    sine = -np.sin(angle, dtype=np.float32) * factor
    dft = np.stack([cosine, sine])
    free = np.where(index < W // 2, index, index - W).astype(np.float32)
    phase = (free[:, None] * free[:, None] + free[None, :] * free[None, :]) * np.float32(math.pi / (4.0 * W))
    kernel = np.stack([np.cos(phase, dtype=np.float32), np.sin(phase, dtype=np.float32)])
    return dft, kernel


def mm(a, b):
    return jnp.dot(a, b, preferred_element_type=F32)


def transform(pairs, right, left):
    across = jnp.concatenate([jnp.concatenate(p, axis=1) for p in pairs], axis=0)
    first = mm(across.astype(BF16), right).astype(BF16)
    spans = [slice(i * W, (i + 1) * W) for i in range(len(pairs))]
    down = jnp.concatenate(
        [
            jnp.concatenate([first[at, :W] for at in spans], axis=1),
            jnp.concatenate([first[at, W:] for at in spans], axis=1),
        ],
        axis=0,
    )
    out = mm(left, down).astype(BF16)
    return [(out[:W, at], out[W:, at]) for at in spans]


def times(a_re, a_im, b_re, b_im):
    a_re, a_im, b_re, b_im = (v.astype(F32) for v in (a_re, a_im, b_re, b_im))
    return a_re * b_re - a_im * b_im, a_re * b_im + a_im * b_re


def conj_times(a_re, a_im, b_re, b_im):
    a_re, a_im, b_re, b_im = (v.astype(F32) for v in (a_re, a_im, b_re, b_im))
    return a_re * b_re + a_im * b_im, a_re * b_im - a_im * b_re


def placing(axis):
    natural = lax.broadcasted_iota(jnp.int32, (128, 128), axis)
    rows = lax.broadcasted_iota(jnp.int32, (128, 128), 1 - axis)
    band, i, ri, r = rows // 16, rows // 8 % 2, rows // 4 % 2, rows % 4
    return (natural == i * 64 + ri * 32 + band * 4 + r).astype(F32).astype(BF16)


def fill(dft, plus, minus):
    for i in range(2):
        at = slice(i * W, (i + 1) * W)
        plus[at, at] = dft[0]
        minus[at, at] = dft[0]
    for ref, a, b in ((plus, dft[1], -dft[1]), (minus, -dft[1], dft[1])):
        ref[:W, W:] = a
        ref[W:, :W] = b


def window_masks(row, col):
    rows = lax.broadcasted_iota(jnp.int32, (W, W), 0)
    cols = lax.broadcasted_iota(jnp.int32, (W, W), 1)
    return rows >= row, cols >= col


def choose_kernel(above, own, east, out):
    col = above[2 + lax.axis_index("yh")]
    left = lax.broadcasted_iota(jnp.int32, (W, W), 1) >= col
    for ri in range(2):
        out[ri] = jnp.where(left, own[ri].astype(F32), east[ri].astype(F32)).astype(BF16)


def patch_kernel(info, mixed, out):
    row, col = info[0], info[1]
    for ri in range(2):
        value = mixed[ri].astype(F32)
        value = pltpu.roll(value, (W - row) % W, 0)
        value = pltpu.roll(value, (W - col) % W, 1)
        out[ri] = value.astype(BF16)


def pick_kernel(ids, src, out):
    for d in range(NYLX * NYH):
        out[d] = src[:, ids[d]]


def forward_kernel(info, blocks, mine, other, dft, kern, all_psi, all_inc, all_far, power, plus, minus):
    first = info[2] == 0
    fill(dft, plus, minus)
    order = placing(0)

    def pair(g):
        psi, inc, far = (ref.at[2 * g : 2 * g + 2] for ref in (all_psi, all_inc, all_far))
        for z in range(NZ):
            piece = blocks[:, g, z].reshape(128, W)
            placed = mm(order, piece).astype(BF16)
            for i in range(2):
                for ri in range(2):
                    at = i * 64 + ri * 32
                    psi[i, ri, z * BAND : (z + 1) * BAND] = placed[at : at + BAND]
        fwd, inv = plus[...], minus[...]
        p0 = [jnp.where(first, mine[ri], other[ri]) for ri in range(2)]
        p1 = [jnp.where(first, other[ri], mine[ri]) for ri in range(2)]
        pairs = range(2)
        spec = transform([times(psi[i, 0], psi[i, 1], *p0) for i in pairs], fwd, inv)
        moved = transform([times(*spec[i], kern[0], kern[1]) for i in pairs], inv, fwd)
        for i in pairs:
            inc[i, 0], inc[i, 1] = moved[i]
        waves = transform([times(*moved[i], *p1) for i in pairs], fwd, inv)
        total = power[...] if g else 0.0
        for i in pairs:
            far[i, 0], far[i, 1] = waves[i]
            f_re, f_im = waves[i][0].astype(F32), waves[i][1].astype(F32)
            total = total + (f_re * f_re + f_im * f_im)
        power[...] = total

    for g in range(2):
        pair(g)


def backward_kernel(info, *refs):
    all_psi, all_inc, all_far, power_a, power_b, patterns, mine, other, dft, kern = refs[:10]
    terms, out, scratch, plus, minus = refs[10:]
    core = info[2]
    first = core == 0
    fill(dft, plus, minus)
    used = info[4].astype(F32)
    back_order = placing(1)

    def pair(g):
        psi, inc, far = (ref.at[2 * g : 2 * g + 2] for ref in (all_psi, all_inc, all_far))
        fwd, inv = plus[...], minus[...]
        p0 = [jnp.where(first, mine[ri], other[ri]) for ri in range(2)]
        p1 = [jnp.where(first, other[ri], mine[ri]) for ri in range(2)]
        double = 2.0 * ((power_a[...] + power_b[...] - patterns[info[3]]) * used)
        pairs = range(2)
        back = transform([[double * far[i, ri].astype(F32) for ri in range(2)] for i in pairs], inv, fwd)
        term1 = [conj_times(inc[i, 0], inc[i, 1], *back[i]) for i in pairs]
        spec = transform([conj_times(*p1, *back[i]) for i in pairs], fwd, inv)
        back = transform([times(*spec[i], kern[0], -kern[1]) for i in pairs], inv, fwd)
        term0 = [conj_times(psi[i, 0], psi[i, 1], *back[i]) for i in pairs]
        for i in pairs:
            for ri, value in enumerate(conj_times(*p0, *back[i])):
                scratch[i, ri] = value.astype(BF16)
        for layer, term in enumerate((term0, term1)):
            slot = core if layer == 0 else 1 - core
            for ri in range(2):
                value = term[0][ri] + term[1][ri]
                terms[slot, ri] = terms[slot, ri] + value if g else value
        for z in range(NZ):
            at = slice(z * BAND, (z + 1) * BAND)
            pieces = [scratch[i, ri, at] for i in range(2) for ri in range(2)]
            piece = mm(back_order, jnp.concatenate(pieces, axis=0)).astype(BF16)
            out[:, g, z] = piece.reshape(NYLX, 16, W)

    for g in range(2):
        pair(g)


def place_kernel(info, own, other, kept, right, low):
    zero = jnp.zeros((W, W), F32)
    parts = [zero] * 4
    for window, at in ((own, 0), (other, 5)):
        row, col = info[at], info[at + 1]
        upper, left = window_masks(row, col)
        value = pltpu.roll(window[...].astype(F32), row, 0)
        value = pltpu.roll(value, col, 1)
        top, down = jnp.where(upper, value, zero), jnp.where(upper, zero, value)
        pieces = [p for v in (top, down) for p in (jnp.where(left, v, zero), jnp.where(left, zero, v))]
        parts = [p + q for p, q in zip(parts, pieces)]
    kept[...], right[...] = parts[0], parts[1]
    low[0], low[1] = parts[2].astype(BF16), parts[3].astype(BF16)


def scan_sum_kernel(src, ids, out):
    wide = NYLX * NYH * 16
    spread_of = lax.broadcasted_iota(jnp.int32, (128, wide), 1) // 16
    expand = (spread_of == lax.broadcasted_iota(jnp.int32, (128, wide), 0)).astype(BF16)
    idrow = jnp.broadcast_to(ids[...], (8, 128)).astype(F32).astype(BF16)
    scan = mm(idrow, expand)[:1]
    target = lax.broadcasted_iota(jnp.int32, (SCANS * 16, wide), 0)
    column = lax.broadcasted_iota(jnp.int32, (SCANS * 16, wide), 1)
    take = (scan == (target // 16).astype(F32)) & (target % 16 == column % 16)
    take = take.astype(BF16)
    for z in range(NZ):
        out[z] = mm(take, src[:, z].reshape(wide, W)).astype(BF16)


def grad_sum_kernel(src, layer, out, packed):
    total = src[0].astype(F32)
    for z in range(1, NZ):
        total += src[z].astype(F32)
    out[...] = total
    object_part = jnp.sum(layer[...] * layer[...])
    probe_part = jnp.sum(total * total)
    lane = lax.broadcasted_iota(jnp.int32, (1, 128), 1)
    packed[...] = jnp.where(lane == 0, object_part, probe_part)


def finish_kernel(
    info, steps, object_norm, probe_norm, packed, layer, other, tiles, before, grad, probe, probe_before, *outs
):
    new_tiles, direction, new_probe, probe_direction, held, fetched, sems, fetch_sem = outs
    fetch = pltpu.make_async_copy(other, fetched, fetch_sem)
    fetch.start()
    totals = jnp.sum(packed[...].reshape(4 * TILES, 128), axis=0, keepdims=True)
    lane = lax.broadcasted_iota(jnp.int32, (1, 128), 1)

    def square(at, count):
        return jnp.sum(jnp.where(lane == at, totals, 0.0), axis=1, keepdims=True) / float(count)

    ratio = square(0, TILES * LAYERS * 2 * W * W) / object_norm[0]
    rate = steps[0].astype(F32) / 1024.0
    copies = []
    for turn in range(LAYERS):
        l = info[2] if turn == 0 else 1 - info[2]
        if turn == 1:
            fetch.wait()
        for ri in range(2):
            turned = ratio * before[0, l, ri] - (layer, fetched)[turn][ri]
            held[1, turn, ri] = turned
            held[0, turn, ri] = tiles[0, l, ri] + rate * turned
            for k, target in enumerate((new_tiles, direction)):
                copies.append(pltpu.make_async_copy(held.at[k, turn, ri], target.at[0, l, ri], sems.at[k, turn, ri]))
                copies[-1].start()
    ratio = square(1, SCANS * MODES * 2 * W * W) / probe_norm[0]
    probe_rate = steps[1].astype(F32) / 16384.0
    for s in range(SCANS):
        for i in range(2):
            for ri in range(2):
                at = ROWS * (4 * s + 2 * i + ri)
                value = ratio * probe_before[s, i, ri] - grad[at : at + ROWS]
                probe_direction[s, i, ri] = value
                new_probe[s, i, ri] = probe[s, i, ri] + probe_rate * value
    for copy in copies:
        copy.wait()


def finish(scalars, arrays):
    spec = pl.BlockSpec(memory_space=VMEM)
    away = pl.BlockSpec(memory_space=pl.ANY)
    return pl.pallas_call(
        finish_kernel,
        grid_spec=pltpu.PrefetchScalarGridSpec(
            num_scalar_prefetch=4,
            grid=(),
            in_specs=[spec, spec, away] + [spec] * (len(arrays) - 3),
            out_specs=[away, away, spec, spec],
            scratch_shapes=[
                VMEM((2, LAYERS, 2, W, W), F32),
                VMEM((2, W, W), F32),
                pltpu.SemaphoreType.DMA((2, LAYERS, 2)),
                pltpu.SemaphoreType.DMA,
            ],
        ),
        out_shape=[shape((1, LAYERS, 2, W, W), F32)] * 2 + [shape((SCANS, 2, 2, ROWS, W), F32)] * 2,
        compiler_params=pltpu.CompilerParams(vmem_limit_bytes=16 << 20),
    )(*scalars, *arrays)


def plain(kernel, out_shape, *arrays):
    spec = pl.BlockSpec(memory_space=VMEM)
    single = not isinstance(out_shape, (list, tuple))
    return pl.pallas_call(
        kernel,
        in_specs=[spec] * len(arrays),
        out_specs=spec if single else [spec] * len(out_shape),
        out_shape=out_shape,
        compiler_params=pltpu.CompilerParams(vmem_limit_bytes=8 << 20),
    )(*arrays)


def shape(dims, dtype):
    return jax.ShapeDtypeStruct(dims, dtype)


def whole(kernel, out_shape, scalars, arrays, scratch=(), limit=8):
    spec = pl.BlockSpec(memory_space=VMEM)
    single = not isinstance(out_shape, (list, tuple))
    return pl.pallas_call(
        kernel,
        grid_spec=pltpu.PrefetchScalarGridSpec(
            num_scalar_prefetch=1,
            grid=(),
            in_specs=[spec] * len(arrays),
            out_specs=spec if single else [spec] * len(out_shape),
            scratch_shapes=list(scratch),
        ),
        out_shape=out_shape,
        compiler_params=pltpu.CompilerParams(vmem_limit_bytes=limit << 20),
    )(scalars, *arrays)


PAIR = (2, 2, W, W)
ALL_BLOCKS = (NYLX, NYH, NZ, 16, W)


MATRIX = VMEM((2 * W, 2 * W), BF16)


def forward(info, blocks, mine, other, consts):
    outs = [shape((4, 2, W, W), BF16)] * 3 + [shape((W, W), F32)]
    return whole(forward_kernel, outs, info, [blocks, mine, other, *consts], [MATRIX] * 2, 24)


def backward(info, psi, inc, far, power_a, power_b, patterns, mine, other, consts):
    outs = [shape(PAIR, F32), shape(ALL_BLOCKS, BF16)]
    arrays = [psi, inc, far, power_a, power_b, patterns, mine, other, *consts]
    return whole(backward_kernel, outs, info, arrays, [VMEM(PAIR, BF16), MATRIX, MATRIX], 24)


def swap(value, axis):
    return lax.ppermute(value, axis, [(0, 1), (1, 0)])


def from_tile(value, distance):
    route = [(t + distance, t) for t in range(TILES) if 0 <= t + distance < TILES]
    return lax.ppermute(value, TILE_AXES, route)


def exchange(value, axes):
    return lax.all_to_all(value, axes, 0, 0, tiled=True)


def spread(value, axes, count):
    return exchange(jnp.broadcast_to(value[None], (count,) + value.shape), axes)


def update(
    object_tiles,
    object_previous,
    probe,
    probe_previous,
    patterns,
    offsets,
    scan_of_slot,
    tile_load,
    step_sizes,
    object_norm_before,
    probe_norm_before,
):
    core = lax.axis_index("c")
    slot = lax.axis_index("yh")
    dft, kern = tables()
    consts = (
        jnp.asarray(dft, BF16),
        jnp.asarray(kern, F32),
    )
    my_offset = lax.dynamic_index_in_dim(offsets, slot, 1, keepdims=False)
    used = (slot < tile_load[0]).astype(jnp.int32)
    twin_offset = lax.dynamic_index_in_dim(offsets, 1 - slot, 1, keepdims=False)
    info = jnp.concatenate(
        [my_offset, jnp.stack([core.astype(jnp.int32), slot.astype(jnp.int32), used]), twin_offset]
    )
    columns = lax.broadcasted_iota(jnp.int32, (1, 1, W), 2)
    lines = lax.broadcasted_iota(jnp.int32, (1, W, 1), 1)
    my_upper, my_left = lines >= my_offset[0], columns >= my_offset[1]

    zeros = jnp.zeros((1, 128), jnp.int32)
    here = 2 * (NX * lax.axis_index("yl") + lax.axis_index("x"))
    row = lax.dynamic_update_slice(zeros, scan_of_slot[None], (0, here))
    rows = [row]
    for d in range(1, NX):
        rows.append(lax.ppermute(row, "x", [((x + d) % NX, x) for x in range(NX)]))
    row = sum(rows[1:], rows[0])
    row = row + swap(row, "yl")
    ids = row[0, : NYLX * NYH]

    own = lax.dynamic_index_in_dim(object_tiles[0], core, 0, keepdims=False).astype(BF16)
    above = from_tile(offsets, -TGX)
    east = from_tile(own, 1)
    chosen = whole(
        choose_kernel, shape((2, W, W), BF16), above.reshape(4), [own, east]
    )
    south = from_tile(chosen, TGX)

    rows = probe.astype(BF16).reshape(SCANS * 16, W)
    banded = spread(rows, "z", NZ).reshape(NZ, SCANS, 16, W)
    picked = whole(pick_kernel, shape((NYLX * NYH, NZ, 16, W), BF16), ids, [banded])
    blocks = exchange(picked, PLANE).reshape(ALL_BLOCKS)

    mixed = jnp.where(my_upper, jnp.where(my_left, own, east), south)
    mine = whole(patch_kernel, shape((2, W, W), BF16), info, [mixed])
    other = swap(mine, "c")

    psi, inc, far, power = forward(info, blocks, mine, other, consts)
    power_other = swap(power, "c")
    terms, probe_terms = backward(info, psi, inc, far, power, power_other, patterns, mine, other, consts)

    summed = terms[0] + swap(terms[1].astype(BF16), "c").astype(F32)
    real = slot == 0
    window = jnp.where(real, summed[0], summed[1])
    twin = swap(jnp.where(real, summed[1], summed[0]).astype(BF16), "yh")
    field = shape((W, W), F32)
    kept, right, low = whole(
        place_kernel, [field, field, shape((2, W, W), BF16)], info, [window, twin]
    )
    from_above = from_tile(low, -TGX).astype(F32)
    kept = kept + from_above[0]
    right = right + from_above[1]
    received = exchange(probe_terms.reshape(NYLX * NYH, NZ, 16, W), PLANE)
    by_scan = plain(scan_sum_kernel, shape((NZ, SCANS * 16, W), BF16), received, row)
    part_grad = kept + from_tile(right.astype(BF16), -1).astype(F32)
    summed = exchange(by_scan, "z")
    probe_grad, packed = plain(
        grad_sum_kernel, [shape((SCANS * 16, W), F32), shape((1, 128), F32)], summed, part_grad
    )
    packed = spread(packed, ("z",) + PLANE + ("c",), 4 * TILES)
    twin_part = swap(part_grad, "yh")
    layer_grad = jnp.stack(
        [jnp.where(real, part_grad, twin_part), jnp.where(real, twin_part, part_grad)]
    )
    other_grad = swap(layer_grad, "c")

    return finish(
        (info, step_sizes, object_norm_before, probe_norm_before),
        (packed, layer_grad, other_grad, object_tiles, object_previous, probe_grad, probe, probe_previous),
    )


def solution(mesh):
    fine = Mesh(mesh.devices.reshape(NZ, NYL, NX, NYH, NC), ("z", "yl", "x", "yh", "c"))
    tile, mode = TILE_AXES, ("yh", "c")
    objects = P(tile, None, None, None, None)
    probes = P(None, mode, None, tile, None)
    return jax.shard_map(
        update,
        mesh=fine,
        in_specs=(
            objects,
            objects,
            probes,
            probes,
            P(tile, None, None),
            P(None, tile),
            P(tile),
            P(tile),
            P(),
            P(),
            P(),
        ),
        out_specs=(objects, objects, probes, probes),
        check_vma=False,
    )
```

```python
import math

import jax
import jax.numpy as jnp
import numpy as np
from jax import lax
from jax.experimental import pallas as pl
from jax.experimental.pallas import tpu as pltpu
from jax.sharding import Mesh, PartitionSpec as P

TGX = 8
LAYERS = 2
MODES = 8
SCANS = 4
W = 256
NZ, NYL, NX, NYH, NC = 8, 2, 4, 2, 2
NYLX = NYL * NX
TILES = NZ * NYLX
ROWS = W // TILES
BAND = NYLX * ROWS
TILE_AXES = ("z", "yl", "x")
PLANE = ("yl", "x", "yh")
VMEM = pltpu.VMEM
F32 = jnp.float32
BF16 = jnp.bfloat16


def tables():
    index = np.arange(W, dtype=np.int64)
    angle = ((index[:, None] * index[None, :]) % W).astype(np.float32) * np.float32(2.0 * math.pi / W)
    factor = np.float32(1.0 / math.sqrt(W))
    cosine = np.cos(angle, dtype=np.float32) * factor
    sine = -np.sin(angle, dtype=np.float32) * factor
    dft = np.stack([cosine, sine])
    free = np.where(index < W // 2, index, index - W).astype(np.float32)
    phase = (free[:, None] * free[:, None] + free[None, :] * free[None, :]) * np.float32(math.pi / (4.0 * W))
    kernel = np.stack([np.cos(phase, dtype=np.float32), np.sin(phase, dtype=np.float32)])
    return dft, kernel


def mm(a, b):
    return jnp.dot(a, b, preferred_element_type=F32)


def transform(pairs, right, left):
    across = jnp.concatenate([jnp.concatenate(p, axis=1) for p in pairs], axis=0)
    first = mm(across.astype(BF16), right).astype(BF16)
    spans = [slice(i * W, (i + 1) * W) for i in range(len(pairs))]
    down = jnp.concatenate(
        [
            jnp.concatenate([first[at, :W] for at in spans], axis=1),
            jnp.concatenate([first[at, W:] for at in spans], axis=1),
        ],
        axis=0,
    )
    out = mm(left, down).astype(BF16)
    return [(out[:W, at], out[W:, at]) for at in spans]


def times(a_re, a_im, b_re, b_im):
    a_re, a_im, b_re, b_im = (v.astype(F32) for v in (a_re, a_im, b_re, b_im))
    return a_re * b_re - a_im * b_im, a_re * b_im + a_im * b_re


def conj_times(a_re, a_im, b_re, b_im):
    a_re, a_im, b_re, b_im = (v.astype(F32) for v in (a_re, a_im, b_re, b_im))
    return a_re * b_re + a_im * b_im, a_re * b_im - a_im * b_re


def placing(axis):
    natural = lax.broadcasted_iota(jnp.int32, (128, 128), axis)
    rows = lax.broadcasted_iota(jnp.int32, (128, 128), 1 - axis)
    band, i, ri, r = rows // 16, rows // 8 % 2, rows // 4 % 2, rows % 4
    return (natural == i * 64 + ri * 32 + band * 4 + r).astype(F32).astype(BF16)


def fill(dft, plus, minus):
    for i in range(2):
        at = slice(i * W, (i + 1) * W)
        plus[at, at] = dft[0]
        minus[at, at] = dft[0]
    for ref, a, b in ((plus, dft[1], -dft[1]), (minus, -dft[1], dft[1])):
        ref[:W, W:] = a
        ref[W:, :W] = b


def window_masks(row, col):
    rows = lax.broadcasted_iota(jnp.int32, (W, W), 0)
    cols = lax.broadcasted_iota(jnp.int32, (W, W), 1)
    return rows >= row, cols >= col


def choose_kernel(above, own, east, out):
    col = above[2 + lax.axis_index("yh")]
    left = lax.broadcasted_iota(jnp.int32, (W, W), 1) >= col
    for ri in range(2):
        out[ri] = jnp.where(left, own[ri].astype(F32), east[ri].astype(F32)).astype(BF16)


def patch_kernel(info, mixed, out):
    row, col = info[0], info[1]
    for ri in range(2):
        value = mixed[ri].astype(F32)
        value = pltpu.roll(value, (W - row) % W, 0)
        value = pltpu.roll(value, (W - col) % W, 1)
        out[ri] = value.astype(BF16)


def pick_kernel(ids, src, out):
    for d in range(NYLX * NYH):
        out[d] = src[:, ids[d]]


def forward_kernel(info, blocks, mine, other, dft, kern, all_psi, all_inc, all_far, power, plus, minus):
    first = info[2] == 0
    fill(dft, plus, minus)
    order = placing(0)

    def pair(g):
        psi, inc, far = (ref.at[2 * g : 2 * g + 2] for ref in (all_psi, all_inc, all_far))
        for z in range(NZ):
            piece = blocks[:, g, z].reshape(128, W)
            placed = mm(order, piece).astype(BF16)
            for i in range(2):
                for ri in range(2):
                    at = i * 64 + ri * 32
                    psi[i, ri, z * BAND : (z + 1) * BAND] = placed[at : at + BAND]
        fwd, inv = plus[...], minus[...]
        p0 = [jnp.where(first, mine[ri], other[ri]) for ri in range(2)]
        p1 = [jnp.where(first, other[ri], mine[ri]) for ri in range(2)]
        pairs = range(2)
        spec = transform([times(psi[i, 0], psi[i, 1], *p0) for i in pairs], fwd, inv)
        moved = transform([times(*spec[i], kern[0], kern[1]) for i in pairs], inv, fwd)
        for i in pairs:
            inc[i, 0], inc[i, 1] = moved[i]
        waves = transform([times(*moved[i], *p1) for i in pairs], fwd, inv)
        total = power[...] if g else 0.0
        for i in pairs:
            far[i, 0], far[i, 1] = waves[i]
            f_re, f_im = waves[i][0].astype(F32), waves[i][1].astype(F32)
            total = total + (f_re * f_re + f_im * f_im)
        power[...] = total

    for g in range(2):
        pair(g)


def backward_kernel(info, *refs):
    all_psi, all_inc, all_far, power_a, power_b, patterns, mine, other, dft, kern = refs[:10]
    terms, out, scratch, plus, minus = refs[10:]
    core = info[2]
    first = core == 0
    fill(dft, plus, minus)
    used = info[4].astype(F32)
    back_order = placing(1)

    def pair(g):
        psi, inc, far = (ref.at[2 * g : 2 * g + 2] for ref in (all_psi, all_inc, all_far))
        fwd, inv = plus[...], minus[...]
        p0 = [jnp.where(first, mine[ri], other[ri]) for ri in range(2)]
        p1 = [jnp.where(first, other[ri], mine[ri]) for ri in range(2)]
        double = 2.0 * ((power_a[...] + power_b[...] - patterns[info[3]]) * used)
        pairs = range(2)
        back = transform([[double * far[i, ri].astype(F32) for ri in range(2)] for i in pairs], inv, fwd)
        term1 = [conj_times(inc[i, 0], inc[i, 1], *back[i]) for i in pairs]
        spec = transform([conj_times(*p1, *back[i]) for i in pairs], fwd, inv)
        back = transform([times(*spec[i], kern[0], -kern[1]) for i in pairs], inv, fwd)
        term0 = [conj_times(psi[i, 0], psi[i, 1], *back[i]) for i in pairs]
        for i in pairs:
            for ri, value in enumerate(conj_times(*p0, *back[i])):
                scratch[i, ri] = value.astype(BF16)
        for layer, term in enumerate((term0, term1)):
            slot = core if layer == 0 else 1 - core
            for ri in range(2):
                value = term[0][ri] + term[1][ri]
                terms[slot, ri] = terms[slot, ri] + value if g else value
        for z in range(NZ):
            at = slice(z * BAND, (z + 1) * BAND)
            pieces = [scratch[i, ri, at] for i in range(2) for ri in range(2)]
            piece = mm(back_order, jnp.concatenate(pieces, axis=0)).astype(BF16)
            out[:, g, z] = piece.reshape(NYLX, 16, W)

    for g in range(2):
        pair(g)


def place_kernel(info, own, other, kept, right, low):
    zero = jnp.zeros((W, W), F32)
    parts = [zero] * 4
    for window, at in ((own, 0), (other, 5)):
        row, col = info[at], info[at + 1]
        upper, left = window_masks(row, col)
        value = pltpu.roll(window[...].astype(F32), row, 0)
        value = pltpu.roll(value, col, 1)
        top, down = jnp.where(upper, value, zero), jnp.where(upper, zero, value)
        pieces = [p for v in (top, down) for p in (jnp.where(left, v, zero), jnp.where(left, zero, v))]
        parts = [p + q for p, q in zip(parts, pieces)]
    kept[...], right[...] = parts[0], parts[1]
    low[0], low[1] = parts[2].astype(BF16), parts[3].astype(BF16)


def scan_sum_kernel(src, ids, out):
    wide = NYLX * NYH * 16
    spread_of = lax.broadcasted_iota(jnp.int32, (128, wide), 1) // 16
    expand = (spread_of == lax.broadcasted_iota(jnp.int32, (128, wide), 0)).astype(BF16)
    idrow = jnp.broadcast_to(ids[...], (8, 128)).astype(F32).astype(BF16)
    scan = mm(idrow, expand)[:1]
    target = lax.broadcasted_iota(jnp.int32, (SCANS * 16, wide), 0)
    column = lax.broadcasted_iota(jnp.int32, (SCANS * 16, wide), 1)
    take = (scan == (target // 16).astype(F32)) & (target % 16 == column % 16)
    take = take.astype(BF16)
    for z in range(NZ):
        out[z] = mm(take, src[:, z].reshape(wide, W)).astype(BF16)


def grad_sum_kernel(src, layer, out, packed):
    total = src[0].astype(F32)
    for z in range(1, NZ):
        total += src[z].astype(F32)
    out[...] = total
    object_part = jnp.sum(layer[...] * layer[...])
    probe_part = jnp.sum(total * total)
    lane = lax.broadcasted_iota(jnp.int32, (1, 128), 1)
    packed[...] = jnp.where(lane == 0, object_part, probe_part)


def finish_kernel(
    info, steps, object_norm, probe_norm, packed, layer, other, tiles, before, grad, probe, probe_before, *outs
):
    new_tiles, direction, new_probe, probe_direction, held, fetched, sems, fetch_sem = outs
    fetch = pltpu.make_async_copy(other, fetched, fetch_sem)
    fetch.start()
    totals = jnp.sum(packed[...].reshape(4 * NYLX, 128), axis=0, keepdims=True)
    lane = lax.broadcasted_iota(jnp.int32, (1, 128), 1)

    def square(at, count):
        return jnp.sum(jnp.where(lane == at, totals, 0.0), axis=1, keepdims=True) / float(count)

    ratio = square(0, TILES * LAYERS * 2 * W * W) / object_norm[0]
    rate = steps[0].astype(F32) / 1024.0
    copies = []
    for turn in range(LAYERS):
        l = info[2] if turn == 0 else 1 - info[2]
        if turn == 1:
            fetch.wait()
        for ri in range(2):
            turned = ratio * before[0, l, ri] - (layer, fetched)[turn][ri]
            held[1, turn, ri] = turned
            held[0, turn, ri] = tiles[0, l, ri] + rate * turned
            for k, target in enumerate((new_tiles, direction)):
                copies.append(pltpu.make_async_copy(held.at[k, turn, ri], target.at[0, l, ri], sems.at[k, turn, ri]))
                copies[-1].start()
    ratio = square(1, SCANS * MODES * 2 * W * W) / probe_norm[0]
    probe_rate = steps[1].astype(F32) / 16384.0
    for s in range(SCANS):
        for i in range(2):
            for ri in range(2):
                at = ROWS * (4 * s + 2 * i + ri)
                value = ratio * probe_before[s, i, ri] - grad[at : at + ROWS]
                probe_direction[s, i, ri] = value
                new_probe[s, i, ri] = probe[s, i, ri] + probe_rate * value
    for copy in copies:
        copy.wait()


def finish(scalars, arrays):
    spec = pl.BlockSpec(memory_space=VMEM)
    away = pl.BlockSpec(memory_space=pl.ANY)
    return pl.pallas_call(
        finish_kernel,
        grid_spec=pltpu.PrefetchScalarGridSpec(
            num_scalar_prefetch=4,
            grid=(),
            in_specs=[spec, spec, away] + [spec] * (len(arrays) - 3),
            out_specs=[away, away, spec, spec],
            scratch_shapes=[
                VMEM((2, LAYERS, 2, W, W), F32),
                VMEM((2, W, W), F32),
                pltpu.SemaphoreType.DMA((2, LAYERS, 2)),
                pltpu.SemaphoreType.DMA,
            ],
        ),
        out_shape=[shape((1, LAYERS, 2, W, W), F32)] * 2 + [shape((SCANS, 2, 2, ROWS, W), F32)] * 2,
        compiler_params=pltpu.CompilerParams(vmem_limit_bytes=16 << 20),
    )(*scalars, *arrays)


def plain(kernel, out_shape, *arrays):
    spec = pl.BlockSpec(memory_space=VMEM)
    single = not isinstance(out_shape, (list, tuple))
    return pl.pallas_call(
        kernel,
        in_specs=[spec] * len(arrays),
        out_specs=spec if single else [spec] * len(out_shape),
        out_shape=out_shape,
        compiler_params=pltpu.CompilerParams(vmem_limit_bytes=8 << 20),
    )(*arrays)


def shape(dims, dtype):
    return jax.ShapeDtypeStruct(dims, dtype)


def whole(kernel, out_shape, scalars, arrays, scratch=(), limit=8):
    spec = pl.BlockSpec(memory_space=VMEM)
    single = not isinstance(out_shape, (list, tuple))
    return pl.pallas_call(
        kernel,
        grid_spec=pltpu.PrefetchScalarGridSpec(
            num_scalar_prefetch=1,
            grid=(),
            in_specs=[spec] * len(arrays),
            out_specs=spec if single else [spec] * len(out_shape),
            scratch_shapes=list(scratch),
        ),
        out_shape=out_shape,
        compiler_params=pltpu.CompilerParams(vmem_limit_bytes=limit << 20),
    )(scalars, *arrays)


PAIR = (2, 2, W, W)
ALL_BLOCKS = (NYLX, NYH, NZ, 16, W)


MATRIX = VMEM((2 * W, 2 * W), BF16)


def forward(info, blocks, mine, other, consts):
    outs = [shape((4, 2, W, W), BF16)] * 3 + [shape((W, W), F32)]
    return whole(forward_kernel, outs, info, [blocks, mine, other, *consts], [MATRIX] * 2, 24)


def backward(info, psi, inc, far, power_a, power_b, patterns, mine, other, consts):
    outs = [shape(PAIR, F32), shape(ALL_BLOCKS, BF16)]
    arrays = [psi, inc, far, power_a, power_b, patterns, mine, other, *consts]
    return whole(backward_kernel, outs, info, arrays, [VMEM(PAIR, BF16), MATRIX, MATRIX], 24)


def swap(value, axis):
    return lax.ppermute(value, axis, [(0, 1), (1, 0)])


def from_tile(value, distance):
    route = [(t + distance, t) for t in range(TILES) if 0 <= t + distance < TILES]
    return lax.ppermute(value, TILE_AXES, route)


def exchange(value, axes):
    return lax.all_to_all(value, axes, 0, 0, tiled=True)


def spread(value, axes, count):
    return exchange(jnp.broadcast_to(value[None], (count,) + value.shape), axes)


def update(
    object_tiles,
    object_previous,
    probe,
    probe_previous,
    patterns,
    offsets,
    scan_of_slot,
    tile_load,
    step_sizes,
    object_norm_before,
    probe_norm_before,
):
    core = lax.axis_index("c")
    slot = lax.axis_index("yh")
    dft, kern = tables()
    consts = (
        jnp.asarray(dft, BF16),
        jnp.asarray(kern, F32),
    )
    my_offset = lax.dynamic_index_in_dim(offsets, slot, 1, keepdims=False)
    used = (slot < tile_load[0]).astype(jnp.int32)
    twin_offset = lax.dynamic_index_in_dim(offsets, 1 - slot, 1, keepdims=False)
    info = jnp.concatenate(
        [my_offset, jnp.stack([core.astype(jnp.int32), slot.astype(jnp.int32), used]), twin_offset]
    )
    columns = lax.broadcasted_iota(jnp.int32, (1, 1, W), 2)
    lines = lax.broadcasted_iota(jnp.int32, (1, W, 1), 1)
    my_upper, my_left = lines >= my_offset[0], columns >= my_offset[1]

    zeros = jnp.zeros((1, 128), jnp.int32)
    here = 2 * (NX * lax.axis_index("yl") + lax.axis_index("x"))
    row = lax.dynamic_update_slice(zeros, scan_of_slot[None], (0, here))
    rows = [row]
    for d in range(1, NX):
        rows.append(lax.ppermute(row, "x", [((x + d) % NX, x) for x in range(NX)]))
    row = sum(rows[1:], rows[0])
    row = row + swap(row, "yl")
    ids = row[0, : NYLX * NYH]

    own = lax.dynamic_index_in_dim(object_tiles[0], core, 0, keepdims=False).astype(BF16)
    above = from_tile(offsets, -TGX)
    east = from_tile(own, 1)
    chosen = whole(
        choose_kernel, shape((2, W, W), BF16), above.reshape(4), [own, east]
    )
    south = from_tile(chosen, TGX)

    rows = probe.astype(BF16).reshape(SCANS * 16, W)
    banded = spread(rows, "z", NZ).reshape(NZ, SCANS, 16, W)
    picked = whole(pick_kernel, shape((NYLX * NYH, NZ, 16, W), BF16), ids, [banded])
    blocks = exchange(picked, PLANE).reshape(ALL_BLOCKS)

    mixed = jnp.where(my_upper, jnp.where(my_left, own, east), south)
    mine = whole(patch_kernel, shape((2, W, W), BF16), info, [mixed])
    other = swap(mine, "c")

    psi, inc, far, power = forward(info, blocks, mine, other, consts)
    power_other = swap(power, "c")
    terms, probe_terms = backward(info, psi, inc, far, power, power_other, patterns, mine, other, consts)

    summed = terms[0] + swap(terms[1].astype(BF16), "c").astype(F32)
    real = slot == 0
    window = jnp.where(real, summed[0], summed[1])
    twin = swap(jnp.where(real, summed[1], summed[0]).astype(BF16), "yh")
    field = shape((W, W), F32)
    kept, right, low = whole(
        place_kernel, [field, field, shape((2, W, W), BF16)], info, [window, twin]
    )
    from_above = from_tile(low, -TGX).astype(F32)
    kept = kept + from_above[0]
    right = right + from_above[1]
    received = exchange(probe_terms.reshape(NYLX * NYH, NZ, 16, W), PLANE)
    by_scan = plain(scan_sum_kernel, shape((NZ, SCANS * 16, W), BF16), received, row)
    part_grad = kept + from_tile(right.astype(BF16), -1).astype(F32)
    summed = exchange(by_scan, "z")
    probe_grad, packed = plain(
        grad_sum_kernel, [shape((SCANS * 16, W), F32), shape((1, 128), F32)], summed, part_grad
    )
    packed = jnp.sum(spread(packed, "z", NZ), axis=0)
    packed = spread(packed, PLANE + ("c",), 4 * NYLX)
    twin_part = swap(part_grad, "yh")
    layer_grad = jnp.stack(
        [jnp.where(real, part_grad, twin_part), jnp.where(real, twin_part, part_grad)]
    )
    other_grad = swap(layer_grad, "c")

    return finish(
        (info, step_sizes, object_norm_before, probe_norm_before),
        (packed, layer_grad, other_grad, object_tiles, object_previous, probe_grad, probe, probe_previous),
    )


def solution(mesh):
    fine = Mesh(mesh.devices.reshape(NZ, NYL, NX, NYH, NC), ("z", "yl", "x", "yh", "c"))
    tile, mode = TILE_AXES, ("yh", "c")
    objects = P(tile, None, None, None, None)
    probes = P(None, mode, None, tile, None)
    return jax.shard_map(
        update,
        mesh=fine,
        in_specs=(
            objects,
            objects,
            probes,
            probes,
            P(tile, None, None),
            P(None, tile),
            P(tile),
            P(tile),
            P(),
            P(),
            P(),
        ),
        out_specs=(objects, objects, probes, probes),
        check_vma=False,
    )
```
